32 devices in a mesh: tm: 8 (over z, x), space: 4 (over y, core).
Axes of the slice: x: 2, y: 2, z: 4, core: 2. Of those that a mesh axis runs over, the one named last changes fastest.
Arguments:
- frames: bfloat16 [32, 16, 128, 128], P('tm', 'space'), may hold values from -6 to 6
- conv_weight: bfloat16 [3456, 128], replicated, may hold values from -0.109375 to 0.109375
- conv_bias: float32 [128], replicated, may hold values from -3 to 3
- projection: float32 [128, 6], replicated, may hold values from -1 to 1
- levels: int32 [6], replicated, may hold values from 3 to 8, as said below
- centres: int32 [8, 16, 768], P(None, 'space', 'tm'), may hold values from 0 to 7, as said below
- code_grad: float32 [8, 16, 768], P(None, 'space', 'tm'), may hold values from -6 to 6
Outputs:
- quantized: float32 [8, 16, 768], P(None, 'space', 'tm')
- weight_grad: float32 [3456, 128], P('tm', 'space')
- projection_grad: float32 [128, 6], replicated
- bias_grad: float32 [128], replicated
The draws below stay inside these ranges and needn't reach their ends.
Inputs may be any that keep to these rules, and one draw needn't show every extreme that they name: Level counts of the FSQ channels; in every draw some channel has 3 levels and some has 8. centres[g, h, q] is below levels[q % 6].
All inputs are finite; a program needn't handle non-finite values.
Results may differ from the reference program's by a relative error of at most 0.0024.
Values may be sent and summed in bfloat16 or wider, within the bound.
A program may use at most 64 MiB of HBM per device.

```python
import jax
import jax.numpy as jnp
from jax import lax

CH = 128
L = 6
W = 128
F = 32
H = 16
TL = 8
LW = 768
KC = 3456


def level_table(key):
    drawn_base = jax.random.randint(jax.random.fold_in(key, 11), (L,), 3, 9)
    channel_order = jax.random.permutation(jax.random.fold_in(key, 12), L)
    return drawn_base.at[channel_order[0]].set(8).at[channel_order[1]].set(3).astype(jnp.int32)


def draw_levels(key, part):
    return level_table(key)


def draw_centres(key, part):
    column_levels = jnp.tile(level_table(key), W)
    return jax.random.randint(jax.random.fold_in(key, 13), (TL, H, LW), 0, column_levels).astype(jnp.int32)


def level_of(own_key, shape, pieces, smallest, top_value):
    level, own = 1.0, jax.random.fold_in(own_key, 6)
    for position, parts in pieces:
        heights = jnp.exp(jax.random.uniform(jax.random.fold_in(own, position), (parts,), jnp.float32, smallest / len(pieces), top_value / len(pieces)))
        level = level * jnp.repeat(heights, shape[position] // parts).reshape([-1 if axis == position else 1 for axis in range(len(shape))])
    return level


def centred(key, dims, spread, bound, pieces=(), kind=jnp.bfloat16):
    entries = jax.random.normal(key, dims, jnp.float32) * spread
    if len(pieces) > 0:
        entries = level_of(key, dims, pieces, -0.22, 0.18) * entries
    return jnp.clip(entries, min=-bound, max=bound).astype(kind)


def setup_inputs(seed: int = 0) -> dict:
    key_list = jax.random.split(jax.random.key(seed), 8)
    frames = centred(key_list[0], (F, H, W, CH), 1.0, 6.0, ((0, 8), (1, 4)))
    conv_weight = centred(key_list[1], (KC, CH), KC ** -0.5, 0.109375)
    conv_bias = centred(key_list[2], (CH,), 0.5, 3.0, (), jnp.float32)
    projection = centred(key_list[3], (CH, L), (CH // 4) ** -0.5, 1.0, (), jnp.float32)
    levels = draw_levels(jax.random.fold_in(key_list[7], 71), 0)
    centres = draw_centres(jax.random.fold_in(key_list[7], 71), 0)
    code_grad = centred(key_list[6], (TL, H, LW), 1.0, 6.0, ((1, 4), (2, 8)), jnp.float32)
    return {"frames": frames, "conv_weight": conv_weight, "conv_bias": conv_bias, "projection": projection, "levels": levels, "centres": centres, "code_grad": code_grad}


offset_scale = 0.45
commit_weight = 0.25
highest = lax.Precision.HIGHEST


def widen_frames(frame_block):
    frame_width = frame_block.shape[2]
    padded = jnp.pad(frame_block, ((0, 0), (1, 1), (1, 1), (0, 0)))
    return jnp.concatenate([padded[:, :, column_shift:column_shift + frame_width] for column_shift in range(3)], axis=3)


def tap_slabs(widened, frame_count, row_count):
    triple = widened.shape[3]
    slabs = []
    for time_tap in range(3):
        for row_tap in range(3):
            slabs.append(widened[time_tap:time_tap + frame_count, row_tap:row_tap + row_count].reshape(-1, triple))
    return slabs


def reference(frames, conv_weight, conv_bias, projection, levels, centres, code_grad):
    channels = frames.shape[3]
    triple = 3 * channels
    cell_count = H * W
    padded_time = jnp.concatenate([frames[:1], frames[:1], frames], 0)

    def forward(group):
        frame_block = lax.dynamic_slice_in_dim(padded_time, (group * 4).astype(jnp.int32), 6, 0)
        slabs = tap_slabs(widen_frames(frame_block), 4, H)
        preact = jnp.zeros((4 * cell_count, channels), jnp.float32) + conv_bias
        for tap_number in range(9):
            preact = preact + jnp.dot(slabs[tap_number], conv_weight[tap_number * triple:(tap_number + 1) * triple], preferred_element_type=jnp.float32)
        activated = lax.optimization_barrier(jax.nn.silu(preact).astype(jnp.bfloat16))
        pooled = activated.astype(jnp.float32).reshape(4, cell_count, channels).sum(0) * 0.25
        return preact, pooled

    group_index = jnp.arange(TL, dtype=jnp.int32)
    preact_all, pooled_all = lax.map(forward, group_index)
    latent = jnp.dot(pooled_all, projection, precision=highest).reshape(TL, H, LW)
    half_range = (levels.astype(jnp.float32) - 1.0) * 0.5
    half_column = jnp.tile(half_range, W)
    quantized = (centres.astype(jnp.float32) - half_column) / half_column
    squashed = jnp.tanh(latent)
    grad_scale = float(F * H * W) ** -0.5
    code_step = (code_grad / half_column + 2.0 * commit_weight * offset_scale * squashed) * offset_scale * (1.0 - squashed * squashed) * grad_scale
    code_step = code_step.reshape(TL, cell_count, L)
    projection_grad = jnp.einsum("gnc,gnl->cl", pooled_all, code_step, precision=highest)
    pooled_grad = jnp.dot(code_step, projection.T, precision=highest)

    def backward(carry, inputs):
        weight_sum, bias_sum = carry
        preact, grad_group, group = inputs
        frame_block = lax.dynamic_slice_in_dim(padded_time, (group * 4).astype(jnp.int32), 6, 0)
        slabs = tap_slabs(widen_frames(frame_block), 4, H)
        sigmoid_pre = jax.nn.sigmoid(preact)
        silu_slope = sigmoid_pre * (1.0 + preact * (1.0 - sigmoid_pre))
        pre_grad = (0.25 * grad_group[None] * silu_slope.reshape(4, cell_count, channels)).reshape(-1, channels)
        low_grad = pre_grad.astype(jnp.bfloat16)
        blocks = jnp.concatenate([lax.dot_general(tap_slab, low_grad, (((0,), (0,)), ((), ())), preferred_element_type=jnp.float32) for tap_slab in slabs], 0)
        return (weight_sum + blocks, bias_sum + pre_grad.sum(0)), None

    start = (jnp.zeros((27 * channels, channels), jnp.float32), jnp.zeros((channels,), jnp.float32))
    final_carry, unused_out = lax.scan(backward, start, (preact_all, pooled_grad, group_index))
    weight_grad, bias_grad = final_carry
    return quantized, weight_grad, projection_grad, bias_grad
```

```python
import functools

import jax
import jax.numpy as jnp
from jax import lax
from jax.experimental import pallas as pl
from jax.experimental.pallas import tpu as pltpu
from jax.sharding import PartitionSpec as P

offset_scale = 0.45
commit_weight = 0.25
highest = lax.Precision.HIGHEST
MESH = pl.DeviceIdType.MESH
f32, bf16 = jnp.float32, jnp.bfloat16
link_type = bf16


def dot(a, b, ca, cb, precision=None):
    return lax.dot_general(
        a, b, (((ca,), (cb,)), ((), ())), preferred_element_type=f32, precision=precision
    )


def per_level(levels_ref, index, count):
    half = jnp.ones(index.shape, f32)
    for j in range(count):
        half = jnp.where(index == j, (levels_ref[j].astype(f32) - 1.0) * 0.5, half)
    return half


def grid_of(T):
    X = max(d for d in range(1, T + 1) if T % d == 0 and d * d <= T)
    return T // X, X


def packed_rows(oc, KT):
    full, rest = KT // 128, KT % 128
    folded = 0 < rest <= 64 and oc % 32 == 0
    return full, rest, folded, full * oc + (oc // 2 if folded else oc if rest else 0)


def block_kernel(
    T, S, scale,
    frames, weight_in, bias_in, proj_in, levels_in, code_in,
    weight_out, small_out,
    xb, weight, bias, proj, levels, code_grad, cg_a, cg_b, cg_c, pscr, part, slope_t, gt, acc, recv1,
    sum2, stage2, recv2, own3, stage3, recv3,
    sm_send, sm_recv, sx_send, sx_recv, sz_send, sz_recv,
    local_sem, token, halo_s, halo_r, cx_s, cx_r, cz_s, cz_r, ss_s, ss_r, sx_s, sx_r, sz_s, sz_r,
    core_s, core_r, y_s, y_r, tm_s, tm_r,
):
    Y = S // 2
    Z, X = grid_of(T)
    F, R, W, C = frames.shape
    L = levels_in.shape[0]
    TILE = code_in.shape[2]
    oc = C // S
    KC = weight_in.shape[0]
    KT = KC // T
    KZ = KT * X
    G = 3 * C
    full, rest, folded, PB = packed_rows(oc, KT)
    cells = R * W
    t = lax.axis_index("tm")
    s = lax.axis_index("space")
    y, core = s // 2, s % 2
    z, x = t // X, t % X
    up_t, dn_t, up_s, dn_s = t < T - 1, t > 0, s < S - 1, s > 0
    up_z, dn_z = z < Z - 1, z > 0
    turn_up = jnp.logical_and(up_t, x == X - 1)
    turn_dn = jnp.logical_and(dn_t, x == 0)

    barrier = pltpu.get_barrier_semaphore()

    def signal(tt, ss, sem=barrier):
        pl.semaphore_signal(sem, inc=1, device_id=(tt, ss), device_id_type=MESH)

    def signal_if(cond, tt, ss, sem=barrier):
        @pl.when(cond)
        def _():
            signal(tt, ss, sem)

    signal_if(turn_up, t + 1, s)
    signal_if(turn_dn, t - 1, s)
    for dx in range(1, X):
        signal(z * X + lax.rem(x + dx, X), s)
    signal_if(up_z, t + X, s)
    signal_if(dn_z, t - X, s)
    for dy in range(1, Y):
        for dx in range(1, X):
            signal(z * X + lax.rem(x + dx, X), lax.rem(y + dy, Y) * 2 + core)
    for d in range(1, S):
        signal(t, lax.rem(s + d, S))

    own = pltpu.make_async_copy(frames, xb.at[2 : 2 + F, 1 : 1 + R], local_sem.at[0])
    first = [
        pltpu.make_async_copy(frames.at[0], xb.at[k, 1 : 1 + R], local_sem.at[1 + k])
        for k in range(2)
    ]
    code_load = pltpu.make_async_copy(code_in, code_grad, local_sem.at[3])
    proj_load = pltpu.make_async_copy(proj_in, proj, local_sem.at[4])
    bias_load = pltpu.make_async_copy(bias_in, bias, local_sem.at[5])
    levels_load = pltpu.make_async_copy(levels_in, levels, local_sem.at[6])
    weight_load = pltpu.make_async_copy(weight_in, weight, local_sem.at[7])
    code_load.start()
    own.start()
    weight_load.start()
    proj_load.start()
    bias_load.start()
    levels_load.start()

    @pl.when(t == 0)
    def _():
        for copy in first:
            copy.start()

    cg_a[...] = jnp.zeros_like(cg_a)
    pscr[...] = jnp.zeros_like(pscr)

    @pl.when(s == 0)
    def _():
        xb[:, 0] = jnp.zeros((F + 2, W, C), bf16)

    @pl.when(s == S - 1)
    def _():
        xb[:, R + 1] = jnp.zeros((F + 2, W, C), bf16)

    code_load.wait()
    for k in range(T):
        cg_a[k // X, k % X, 0:R, 0:TILE] = code_grad[k]
    cg_b[0] = cg_a[:, x]

    one = lambda c: jnp.where(c, 1, 0)
    pl.semaphore_wait(
        barrier,
        (S - 1) + (X - 1) * Y + one(up_z) + one(dn_z) + one(turn_up) + one(turn_dn),
    )

    def remote(src, dst, ss_, rs_, tt, sp):
        return pltpu.make_async_remote_copy(
            src_ref=src, dst_ref=dst, send_sem=ss_, recv_sem=rs_,
            device_id=(tt, sp), device_id_type=MESH,
        )

    def start_if(cond, copy):
        @pl.when(cond)
        def _():
            copy.start()

    def recv_if(cond, copy):
        @pl.when(cond)
        def _():
            copy.wait_recv()

    def sent_if(cond, copy):
        @pl.when(cond)
        def _():
            copy.wait_send()

    def cgx_copy(d):
        to = lax.rem(x + d, X)
        return remote(cg_a.at[:, to], cg_b.at[d], cx_s.at[d], cx_r.at[d], z * X + to, s)

    def cgz_copy(d):
        to = lax.rem(z + d, Z)
        return remote(cg_b.at[:, to], cg_c.at[d], cz_s.at[d], cz_r.at[d], to * X + x, s)

    H = R + 1

    def halo(k, src, dst, tt, sp):
        return remote(src, dst, halo_s.at[k], halo_r.at[k], tt, sp)

    row_up = halo(0, frames.at[:, R - 1], xb.at[2 : 2 + F, 0], t, s + 1)
    row_dn = halo(1, frames.at[:, 0], xb.at[2 : 2 + F, H], t, s - 1)
    edge_lo = halo(2, frames.at[F - 2 : F, 0], xb.at[0:2, 1], t + 1, s)
    edge_hi = halo(3, frames.at[F - 2 : F, R - 1], xb.at[0:2, R], t + 1, s)
    inner = halo(4, frames.at[F - 2 : F, 1 : R - 1], xb.at[0:2, 2:R], t + 1, s)
    pass_dn = halo(5, xb.at[0:2, 1], xb.at[0:2, H], t, s - 1)
    pass_up = halo(6, xb.at[0:2, R], xb.at[0:2, 0], t, s + 1)
    late_dn, late_up = jnp.logical_and(dn_t, dn_s), jnp.logical_and(dn_t, up_s)

    for d in range(1, X):
        cgx_copy(d).start()
    start_if(up_t, edge_lo)
    start_if(up_t, edge_hi)
    start_if(up_s, row_up)
    start_if(dn_s, row_dn)

    def token_send(r):
        signal_if(up_z, t + X, s, token.at[r, 0])
        signal_if(dn_z, t - X, s, token.at[r, 1])

    def token_wait(r):
        @pl.when(dn_z)
        def _():
            pl.semaphore_wait(token.at[r, 0], 1)

        @pl.when(up_z)
        def _():
            pl.semaphore_wait(token.at[r, 1], 1)

    for r in range(max(Z - 2, 0)):
        token_send(r)
        token_wait(r)
    for d in range(1, X):
        cgx_copy(d).wait_recv()
    for d in range(1, Z):
        cgz_copy(d).start()
    start_if(up_t, inner)

    proj_load.wait()
    bias_load.wait()
    levels_load.wait()
    pscr[0:L] = proj[...]
    proj_t = pscr[...]
    row = lax.broadcasted_iota(jnp.int32, (cells, C), 0) % W

    def taps(f, times):
        slabs = []
        weights = []
        for a in times:
            for b in range(3):
                slabs.append(xb[f + a, b : b + R].reshape(cells, C))
                k0 = (a * 3 + b) * G
                weights.append(
                    jnp.concatenate([weight[k0 + c * C : k0 + (c + 1) * C] for c in range(3)], 1)
                )
        return dot(jnp.concatenate(slabs, 1), jnp.concatenate(weights, 0), 1, 0)

    def frame_end(f, out):
        left = jnp.where(row == 0, 0.0, pltpu.roll(out[:, 0:C], 1, 0))
        right = jnp.where(row == W - 1, 0.0, pltpu.roll(out[:, 2 * C :], cells - 1, 0))
        pre = out[:, C : 2 * C] + bias[...] + left + right
        sig = 1.0 / (1.0 + jnp.exp(-pre))
        act = (pre * sig).astype(bf16).astype(f32)
        slope = sig * (1.0 + pre * (1.0 - sig))
        for h in range(R):
            slope_t[f * R + h] = slope[h * W : (h + 1) * W].T
        return act

    own.wait()
    weight_load.wait()
    recv_if(dn_s, row_up)
    recv_if(up_s, row_dn)
    pooled = frame_end(2, taps(2, (0, 1, 2)))

    recv_if(dn_t, edge_lo)
    start_if(late_dn, pass_dn)
    recv_if(dn_t, edge_hi)
    start_if(late_up, pass_up)
    pooled = pooled + frame_end(3, taps(3, (0, 1, 2)))
    part[0] = taps(0, (2,))
    part[1] = taps(1, (1, 2))

    cg_c[0] = cg_b[:, z]
    for d in range(1, Z):
        cgz_copy(d).wait_recv()
    wt = TILE // L
    cg_all = cg_c[...].reshape(T * 8, 128)
    r_i = lax.broadcasted_iota(jnp.int32, (T * 8, cells), 0)
    q_i = lax.broadcasted_iota(jnp.int32, (T * 8, cells), 1)
    piece = r_i // 8
    owner = lax.rem(z - piece // X + Z, Z) * X + lax.rem(x - piece % X + X, X)
    pick = jnp.logical_and(r_i % 8 == q_i // W, owner == (q_i % W) // wt).astype(f32)
    spread = dot(cg_all, pick, 0, 0, highest)
    l_i = lax.broadcasted_iota(jnp.int32, (128, cells), 0)
    w_i = lax.broadcasted_iota(jnp.int32, (128, cells), 1) % W
    spread = jnp.where(jnp.logical_and(l_i // L == w_i % wt, l_i < TILE), spread, 0.0)
    j_i = lax.broadcasted_iota(jnp.int32, (8, 128), 0)
    m_i = lax.broadcasted_iota(jnp.int32, (8, 128), 1)
    fold = jnp.logical_and(m_i % L == j_i, m_i < TILE).astype(f32)
    code = dot(fold, spread, 1, 0, highest)
    half_j = per_level(levels, lax.broadcasted_iota(jnp.int32, (8, cells), 0), L)
    code = code / half_j

    @pl.when(t == 0)
    def _():
        for k in range(2):
            first[k].wait()
            xb[k, 0] = xb[2, 0]
            xb[k, H] = xb[2, H]

    recv_if(dn_t, inner)
    recv_if(late_up, pass_dn)
    recv_if(late_dn, pass_up)
    pooled = pooled + frame_end(0, part[0] + taps(0, (0, 1)))
    pooled = (pooled + frame_end(1, part[1] + taps(1, (0,)))) * 0.25

    latent = dot(proj_t, pooled, 1, 1, highest)
    squashed = jnp.tanh(latent)
    step = (
        (code + 2.0 * commit_weight * offset_scale * squashed)
        * offset_scale
        * (1.0 - squashed * squashed)
        * scale
    )
    proj_part = dot(step, pooled, 1, 0, highest)
    pg_t = dot(proj_t, step, 0, 0, highest) * 0.25

    lane = lax.broadcasted_iota(jnp.int32, (C, W), 1)
    bias_sum = jnp.zeros((C, W), f32)
    for f in range(F):
        for h in range(R):
            g = pg_t[:, h * W : (h + 1) * W] * slope_t[f * R + h]
            bias_sum = bias_sum + g
            q0 = (f * R + h) * W
            gt[0:C, q0 : q0 + W] = jnp.where(lane == W - 1, 0.0, pltpu.roll(g, W - 1, 1)).astype(bf16)
            gt[C : 2 * C, q0 : q0 + W] = g.astype(bf16)
            gt[2 * C :, q0 : q0 + W] = jnp.where(lane == 0, 0.0, pltpu.roll(g, 1, 1)).astype(bf16)

    def small_space(d):
        return remote(sm_send, sm_recv.at[d], ss_s.at[d], ss_r.at[d], t, lax.rem(s + d, S))

    def small_x(d):
        return remote(sx_send, sx_recv.at[d], sx_s.at[d], sx_r.at[d], z * X + lax.rem(x + d, X), s)

    def small_z(d):
        return remote(sz_send, sz_recv.at[d], sz_s.at[d], sz_r.at[d], lax.rem(z + d, Z) * X + x, s)

    def core_copy(g):
        lanes = slice(g * G, (g + 1) * G)
        return remote(
            acc.at[1 - core, :, :, lanes], recv1.at[:, :, lanes],
            core_s.at[g], core_r.at[g], t, s + 1 - 2 * core,
        )

    def plane_copy(c, dy, dx):
        ty, tx, k = lax.rem(y + dy, Y), lax.rem(x + dx, X), dy * X + dx
        return remote(
            stage2.at[c, ty, tx], recv2.at[c, k], y_s.at[c, k], y_r.at[c, k],
            z * X + tx, ty * 2 + core,
        )

    def z_copy(to, slot):
        return remote(stage3.at[to], recv3.at[slot], tm_s.at[to], tm_r.at[slot], to * X + x, s)

    peers = [(dy, dx) for dy in range(Y) for dx in range(X) if dy or dx]
    chunks = sorted(range(Z), key=lambda c: -max(c, Z - 1 - c))

    def groups_of(c):
        return range(c * KZ // G, ((c + 1) * KZ - 1) // G + 1)

    order = []
    for c in chunks:
        order += [g for g in groups_of(c) if g not in order]
    sets = [order[k : k + 2] for k in range(0, len(order), 2)]

    def products(groups):
        rhs = jnp.concatenate(
            [xb[g // 3 : g // 3 + F, g % 3 : g % 3 + R].reshape(F * cells, C) for g in groups], 1
        )
        res = dot(gt[...], rhs, 1, 0)
        for n, g in enumerate(groups):
            for c in range(3):
                k0 = g * G + c * C
                for sp in range(S):
                    acc[sp % 2, sp // 2, :, k0 : k0 + C] = res[
                        c * C + sp * oc : c * C + (sp + 1) * oc, n * C : (n + 1) * C
                    ]
            core_copy(g).start()

    half_lane = lax.broadcasted_iota(jnp.int32, (oc // 2, 128), 1) < 64
    arrived = set()

    def fold_core(c):
        for g in groups_of(c):
            if g not in arrived:
                core_copy(g).wait_recv()
                arrived.add(g)
        for yy in range(Y):
            for xx in range(X):
                off = (c * X + xx) * KT
                base = off // 128 * 128
                wide = min(-(-KT // 128) * 128 + 128, KC - base)
                win = acc[core, yy, :, base : base + wide] + recv1[yy, :, base : base + wide]
                if off > base:
                    win = pltpu.roll(win, wide - (off - base), 1)
                pieces = [win[:, 128 * k : 128 * (k + 1)] for k in range(full)]
                if rest:
                    last = win[:, 128 * full : 128 * (full + 1)]
                    if folded:
                        last = jnp.where(
                            half_lane, last[: oc // 2], pltpu.roll(last[oc // 2 :], 64, 1)
                        )
                    pieces.append(last)
                block = jnp.concatenate(pieces, 0)
                sum2[c, yy, xx] = block
                stage2[c, yy, xx] = block.astype(link_type)
        for dy, dx in peers:
            plane_copy(c, dy, dx).start()

    def fold_plane(c):
        v = sum2[c, y, x]
        for dy, dx in peers:
            plane_copy(c, dy, dx).wait_recv()
            v = v + recv2[c, dy * X + dx].astype(f32)
        own3[c] = v
        stage3[c] = v.astype(link_type)
        start_if(z != c, z_copy(c, z))

    bias_part = dot(jnp.ones((8, W), f32), bias_sum, 1, 1, highest)
    sm_send[...] = jnp.where(lax.broadcasted_iota(jnp.int32, (8, C), 0) == L, bias_part, proj_part)
    for d in range(1, S):
        small_space(d).start()

    ready = {}
    computed = []
    waiting = list(chunks)
    for n, groups in enumerate(sets):
        products(groups)
        if ready.get("next") is not None:
            fold_core(ready.pop("next"))
        computed += groups
        if waiting and all(g in computed for g in groups_of(waiting[0])):
            ready["next"] = waiting.pop(0)
    if ready.get("next") is not None:
        fold_core(ready.pop("next"))
    for c in waiting:
        fold_core(c)

    sm = sm_send[...]
    for d in range(1, S):
        small_space(d).wait_recv()
        sm = sm + sm_recv[d]
    sx_send[...] = sm
    for d in range(1, X):
        small_x(d).start()
    for n, c in enumerate(chunks):
        fold_plane(c)
        if n == 0:
            for d in range(1, X):
                small_x(d).wait_recv()
                sm = sm + sx_recv[d]
            sz_send[...] = sm
            for d in range(1, Z):
                small_z(d).start()
    for d in range(1, Z):
        small_z(d).wait_recv()
        sm = sm + sz_recv[d]
    small_out[...] = sm

    res = own3[z]
    for d in range(1, Z):
        src = lax.rem(z + d, Z)
        z_copy(src, src).wait_recv()
        res = res + recv3[src].astype(f32)
    for k in range(full):
        weight_out[:, 128 * k : 128 * (k + 1)] = res[k * oc : (k + 1) * oc]
    if rest:
        last = res[full * oc :]
        if folded:
            last = jnp.concatenate([last, pltpu.roll(last, 64, 1)], 0)
        weight_out[:, 128 * full :] = last[:, :rest]

    sent_if(up_s, row_up)
    sent_if(dn_s, row_dn)
    for copy in (edge_lo, edge_hi, inner):
        sent_if(up_t, copy)
    sent_if(late_dn, pass_dn)
    sent_if(late_up, pass_up)
    for d in range(1, X):
        cgx_copy(d).wait_send()
        small_x(d).wait_send()
    for d in range(1, Z):
        cgz_copy(d).wait_send()
        small_z(d).wait_send()
    for d in range(1, S):
        small_space(d).wait_send()
    for g in range(KC // G):
        core_copy(g).wait_send()
    for c in range(Z):
        for dy, dx in peers:
            plane_copy(c, dy, dx).wait_send()
        sent_if(z != c, z_copy(c, z))


def finish_kernel(levels, centres, wg, small, quant_out, weight_out, proj_out, bias_out):
    L = levels.shape[0]
    lane = lax.broadcasted_iota(jnp.int32, centres.shape, 2)
    half = per_level(levels, lax.rem(lane, L), L)
    quant_out[...] = (centres[...].astype(f32) - half) / half
    weight_out[...] = wg[...]
    proj_out[...] = small[0:L]
    bias_out[...] = small[L : L + 1]


def on_device(T, S, frames, conv_weight, conv_bias, projection, levels, centres, code_grad):
    F, R, W, C = frames.shape
    KC = conv_weight.shape[0]
    KT = KC // T
    oc, Y, cells = C // S, S // 2, R * W
    Z, X = grid_of(T)
    PB = packed_rows(oc, KT)[3]
    L, TILE = levels.shape[0], code_grad.shape[2]
    scale = float(F * T * R * S * W) ** -0.5
    vmem = pl.BlockSpec(memory_space=pltpu.VMEM)
    dma = pltpu.SemaphoreType.DMA
    wg, small = pl.pallas_call(
        functools.partial(block_kernel, T, S, scale),
        out_shape=(
            jax.ShapeDtypeStruct((oc, KT), f32),
            jax.ShapeDtypeStruct((8, C), f32),
        ),
        in_specs=[pl.BlockSpec(memory_space=pl.ANY)] * 6,
        out_specs=(vmem, vmem),
        scratch_shapes=[
            pltpu.VMEM((F + 2, R + 2, W, C), bf16),
            pltpu.VMEM((KC, C), bf16),
            pltpu.VMEM((1, C), f32),
            pltpu.VMEM((L, C), f32),
            pltpu.SMEM((L,), jnp.int32),
            pltpu.VMEM((T, R, TILE), f32),
            pltpu.VMEM((Z, X, 8, 128), f32),
            pltpu.VMEM((X, Z, 8, 128), f32),
            pltpu.VMEM((Z, X, 8, 128), f32),
            pltpu.VMEM((8, C), f32),
            pltpu.VMEM((2, cells, 3 * C), f32),
            pltpu.VMEM((F * R, C, W), f32),
            pltpu.VMEM((3 * C, F * cells), bf16),
            pltpu.VMEM((2, Y, oc, KC), f32),
            pltpu.VMEM((Y, oc, KC), f32),
            pltpu.VMEM((Z, Y, X, PB, 128), f32),
            pltpu.VMEM((Z, Y, X, PB, 128), link_type),
            pltpu.VMEM((Z, Y * X, PB, 128), link_type),
            pltpu.VMEM((Z, PB, 128), f32),
            pltpu.VMEM((Z, PB, 128), link_type),
            pltpu.VMEM((Z, PB, 128), link_type),
            pltpu.VMEM((8, C), f32),
            pltpu.VMEM((S, 8, C), f32),
            pltpu.VMEM((8, C), f32),
            pltpu.VMEM((X, 8, C), f32),
            pltpu.VMEM((8, C), f32),
            pltpu.VMEM((Z, 8, C), f32),
            dma((8,)), pltpu.SemaphoreType.REGULAR((max(Z - 2, 1), 2)),
            dma((7,)), dma((7,)), dma((X,)), dma((X,)), dma((Z,)), dma((Z,)),
            dma((S,)), dma((S,)), dma((X,)), dma((X,)), dma((Z,)), dma((Z,)),
            dma((9,)), dma((9,)), dma((Z, Y * X)), dma((Z, Y * X)), dma((Z,)), dma((Z,)),
        ],
        compiler_params=pltpu.CompilerParams(
            collective_id=0, has_side_effects=True, vmem_limit_bytes=56 * 1024 * 1024
        ),
    )(frames, conv_weight, conv_bias.reshape(1, C), projection.T, levels, code_grad)
    quantized, wg, proj_grad, bias_grad = pl.pallas_call(
        finish_kernel,
        out_shape=(
            jax.ShapeDtypeStruct(centres.shape, f32),
            jax.ShapeDtypeStruct(wg.shape, f32),
            jax.ShapeDtypeStruct((L, C), f32),
            jax.ShapeDtypeStruct((1, C), f32),
        ),
        in_specs=[pl.BlockSpec(memory_space=pltpu.SMEM), vmem, vmem, vmem],
        out_specs=(vmem,) * 4,
    )(levels, centres, wg, small)
    return quantized, wg.T, proj_grad.T, bias_grad.reshape(C)


def solution(mesh):
    return jax.shard_map(
        functools.partial(on_device, mesh.shape["tm"], mesh.shape["space"]),
        mesh=mesh,
        in_specs=(
            P("tm", "space", None, None),
            P(),
            P(),
            P(),
            P(),
            P(None, "space", "tm"),
            P(None, "space", "tm"),
        ),
        out_specs=(P(None, "space", "tm"), P("tm", "space"), P(), P()),
        check_vma=False,
    )
```

```python
import functools

import jax
import jax.numpy as jnp
from jax import lax
from jax.experimental import pallas as pl
from jax.experimental.pallas import tpu as pltpu
from jax.sharding import PartitionSpec as P

offset_scale = 0.45
commit_weight = 0.25
highest = lax.Precision.HIGHEST
MESH = pl.DeviceIdType.MESH
f32, bf16 = jnp.float32, jnp.bfloat16
link_type = bf16


def dot(a, b, ca, cb, precision=None):
    return lax.dot_general(
        a, b, (((ca,), (cb,)), ((), ())), preferred_element_type=f32, precision=precision
    )


def per_level(levels_ref, index, count):
    half = jnp.ones(index.shape, f32)
    for j in range(count):
        half = jnp.where(index == j, (levels_ref[j].astype(f32) - 1.0) * 0.5, half)
    return half


def grid_of(T):
    X = max(d for d in range(1, T + 1) if T % d == 0 and d * d <= T)
    return T // X, X


def packed_rows(oc, KT):
    full, rest = KT // 128, KT % 128
    folded = 0 < rest <= 64 and oc % 32 == 0
    return full, rest, folded, full * oc + (oc // 2 if folded else oc if rest else 0)


def block_kernel(
    T, S, scale,
    frames, weight_in, bias_in, proj_in, levels_in, code_in,
    weight_out, small_out,
    xb, weight, bias, proj, levels, code_grad, cg_a, cg_b, cg_c, pscr, part, slope_t, gt, acc, recv1,
    sum2, stage2, recv2, own3, stage3, recv3,
    sm_send, sm_recv, sz_send, sz_recv,
    local_sem, token, halo_s, halo_r, cx_s, cx_r, cz_s, cz_r, ss_s, ss_r, sz_s, sz_r,
    core_s, core_r, y_s, y_r, tm_s, tm_r,
):
    Y = S // 2
    Z, X = grid_of(T)
    F, R, W, C = frames.shape
    L = levels_in.shape[0]
    TILE = code_in.shape[2]
    oc = C // S
    KC = weight_in.shape[0]
    KT = KC // T
    KZ = KT * X
    G = 3 * C
    full, rest, folded, PB = packed_rows(oc, KT)
    cells = R * W
    t = lax.axis_index("tm")
    s = lax.axis_index("space")
    y, core = s // 2, s % 2
    z, x = t // X, t % X
    up_t, dn_t, up_s, dn_s = t < T - 1, t > 0, s < S - 1, s > 0
    up_z, dn_z = z < Z - 1, z > 0
    turn_up = jnp.logical_and(up_t, x == X - 1)
    turn_dn = jnp.logical_and(dn_t, x == 0)

    barrier = pltpu.get_barrier_semaphore()

    def signal(tt, ss, sem=barrier):
        pl.semaphore_signal(sem, inc=1, device_id=(tt, ss), device_id_type=MESH)

    def signal_if(cond, tt, ss, sem=barrier):
        @pl.when(cond)
        def _():
            signal(tt, ss, sem)

    signal_if(turn_up, t + 1, s)
    signal_if(turn_dn, t - 1, s)
    signal_if(up_z, t + X, s)
    signal_if(dn_z, t - X, s)
    plane = [(dx, ds) for dx in range(X) for ds in range(S) if dx or ds]
    for dx, ds in plane:
        signal(z * X + lax.rem(x + dx, X), lax.rem(s + ds, S))

    own = pltpu.make_async_copy(frames, xb.at[2 : 2 + F, 1 : 1 + R], local_sem.at[0])
    first = [
        pltpu.make_async_copy(frames.at[0], xb.at[k, 1 : 1 + R], local_sem.at[1 + k])
        for k in range(2)
    ]
    code_load = pltpu.make_async_copy(code_in, code_grad, local_sem.at[3])
    proj_load = pltpu.make_async_copy(proj_in, proj, local_sem.at[4])
    bias_load = pltpu.make_async_copy(bias_in, bias, local_sem.at[5])
    levels_load = pltpu.make_async_copy(levels_in, levels, local_sem.at[6])
    weight_load = pltpu.make_async_copy(weight_in, weight, local_sem.at[7])
    code_load.start()
    own.start()
    weight_load.start()
    proj_load.start()
    bias_load.start()
    levels_load.start()

    @pl.when(t == 0)
    def _():
        for copy in first:
            copy.start()

    cg_a[...] = jnp.zeros_like(cg_a)
    pscr[...] = jnp.zeros_like(pscr)

    @pl.when(s == 0)
    def _():
        xb[:, 0] = jnp.zeros((F + 2, W, C), bf16)

    @pl.when(s == S - 1)
    def _():
        xb[:, R + 1] = jnp.zeros((F + 2, W, C), bf16)

    code_load.wait()
    for k in range(T):
        cg_a[k // X, k % X, 0:R, 0:TILE] = code_grad[k]
    cg_b[0] = cg_a[:, x]

    one = lambda c: jnp.where(c, 1, 0)
    pl.semaphore_wait(
        barrier,
        (S * X - 1) + one(up_z) + one(dn_z) + one(turn_up) + one(turn_dn),
    )

    def remote(src, dst, ss_, rs_, tt, sp):
        return pltpu.make_async_remote_copy(
            src_ref=src, dst_ref=dst, send_sem=ss_, recv_sem=rs_,
            device_id=(tt, sp), device_id_type=MESH,
        )

    def start_if(cond, copy):
        @pl.when(cond)
        def _():
            copy.start()

    def recv_if(cond, copy):
        @pl.when(cond)
        def _():
            copy.wait_recv()

    def sent_if(cond, copy):
        @pl.when(cond)
        def _():
            copy.wait_send()

    def cgx_copy(d):
        to = lax.rem(x + d, X)
        return remote(cg_a.at[:, to], cg_b.at[d], cx_s.at[d], cx_r.at[d], z * X + to, s)

    def cgz_copy(d):
        to = lax.rem(z + d, Z)
        return remote(cg_b.at[:, to], cg_c.at[d], cz_s.at[d], cz_r.at[d], to * X + x, s)

    H = R + 1

    def halo(k, src, dst, tt, sp):
        return remote(src, dst, halo_s.at[k], halo_r.at[k], tt, sp)

    row_up = halo(0, frames.at[:, R - 1], xb.at[2 : 2 + F, 0], t, s + 1)
    row_dn = halo(1, frames.at[:, 0], xb.at[2 : 2 + F, H], t, s - 1)
    edge_lo = halo(2, frames.at[F - 2 : F, 0], xb.at[0:2, 1], t + 1, s)
    edge_hi = halo(3, frames.at[F - 2 : F, R - 1], xb.at[0:2, R], t + 1, s)
    inner = halo(4, frames.at[F - 2 : F, 1 : R - 1], xb.at[0:2, 2:R], t + 1, s)
    pass_dn = halo(5, xb.at[0:2, 1], xb.at[0:2, H], t, s - 1)
    pass_up = halo(6, xb.at[0:2, R], xb.at[0:2, 0], t, s + 1)
    late_dn, late_up = jnp.logical_and(dn_t, dn_s), jnp.logical_and(dn_t, up_s)

    rounds = max(Z - 2, 0)

    def chain(side):
        sends, gets, to = ((up_z, dn_z, t + X), (dn_z, up_z, t - X))[side]
        for r in range(rounds):
            @pl.when(gets)
            def _():
                pl.semaphore_wait(token.at[r, side], 1)

            if r + 1 < rounds:
                signal_if(sends, to, s, token.at[r + 1, side])

    def cgz_start(upper):
        for d in range(1, Z):
            above = lax.rem(z + d, Z) > z
            start_if(above if upper else jnp.logical_not(above), cgz_copy(d))

    if rounds:
        signal_if(up_z, t + X, s, token.at[0, 0])
        signal_if(dn_z, t - X, s, token.at[0, 1])
    for d in range(1, X):
        cgx_copy(d).start()
    start_if(up_t, edge_lo)
    start_if(up_t, edge_hi)
    start_if(up_s, row_up)
    start_if(dn_s, row_dn)
    sent_if(up_t, edge_lo)
    sent_if(up_t, edge_hi)
    start_if(up_t, inner)
    proj_load.wait()
    bias_load.wait()
    levels_load.wait()
    pscr[0:L] = proj[...]
    proj_t = pscr[...]
    row = lax.broadcasted_iota(jnp.int32, (cells, C), 0) % W

    def taps(f, times):
        slabs = []
        weights = []
        for a in times:
            for b in range(3):
                slabs.append(xb[f + a, b : b + R].reshape(cells, C))
                k0 = (a * 3 + b) * G
                weights.append(
                    jnp.concatenate([weight[k0 + c * C : k0 + (c + 1) * C] for c in range(3)], 1)
                )
        return dot(jnp.concatenate(slabs, 1), jnp.concatenate(weights, 0), 1, 0)

    def frame_end(f, out):
        left = jnp.where(row == 0, 0.0, pltpu.roll(out[:, 0:C], 1, 0))
        right = jnp.where(row == W - 1, 0.0, pltpu.roll(out[:, 2 * C :], cells - 1, 0))
        pre = out[:, C : 2 * C] + bias[...] + left + right
        sig = 1.0 / (1.0 + jnp.exp(-pre))
        act = (pre * sig).astype(bf16).astype(f32)
        slope = sig * (1.0 + pre * (1.0 - sig))
        for h in range(R):
            slope_t[f * R + h] = slope[h * W : (h + 1) * W].T
        return act

    own.wait()
    weight_load.wait()
    recv_if(dn_s, row_up)
    recv_if(up_s, row_dn)
    pooled = frame_end(2, taps(2, (0, 1, 2)))

    chain(0)
    for d in range(1, X):
        cgx_copy(d).wait_recv()
    cgz_start(False)
    chain(1)
    cgz_start(True)
    recv_if(dn_t, edge_lo)
    start_if(late_dn, pass_dn)
    recv_if(dn_t, edge_hi)
    start_if(late_up, pass_up)
    pooled = pooled + frame_end(3, taps(3, (0, 1, 2)))
    part[0] = taps(0, (2,))
    part[1] = taps(1, (1, 2))

    @pl.when(t == 0)
    def _():
        for k in range(2):
            first[k].wait()
            xb[k, 0] = xb[2, 0]
            xb[k, H] = xb[2, H]

    recv_if(dn_t, inner)
    recv_if(late_up, pass_dn)
    recv_if(late_dn, pass_up)
    pooled = pooled + frame_end(0, part[0] + taps(0, (0, 1)))
    pooled = (pooled + frame_end(1, part[1] + taps(1, (0,)))) * 0.25

    latent = dot(proj_t, pooled, 1, 1, highest)
    cg_c[0] = cg_b[:, z]
    for d in range(1, Z):
        cgz_copy(d).wait_recv()
    wt = TILE // L
    cg_all = cg_c[...].reshape(T * 8, 128)
    r_i = lax.broadcasted_iota(jnp.int32, (T * 8, cells), 0)
    q_i = lax.broadcasted_iota(jnp.int32, (T * 8, cells), 1)
    piece = r_i // 8
    owner = lax.rem(z - piece // X + Z, Z) * X + lax.rem(x - piece % X + X, X)
    pick = jnp.logical_and(r_i % 8 == q_i // W, owner == (q_i % W) // wt).astype(f32)
    spread = dot(cg_all, pick, 0, 0, highest)
    l_i = lax.broadcasted_iota(jnp.int32, (128, cells), 0)
    w_i = lax.broadcasted_iota(jnp.int32, (128, cells), 1) % W
    spread = jnp.where(jnp.logical_and(l_i // L == w_i % wt, l_i < TILE), spread, 0.0)
    j_i = lax.broadcasted_iota(jnp.int32, (8, 128), 0)
    m_i = lax.broadcasted_iota(jnp.int32, (8, 128), 1)
    fold = jnp.logical_and(m_i % L == j_i, m_i < TILE).astype(f32)
    code = dot(fold, spread, 1, 0, highest)
    half_j = per_level(levels, lax.broadcasted_iota(jnp.int32, (8, cells), 0), L)
    code = code / half_j

    squashed = jnp.tanh(latent)
    step = (
        (code + 2.0 * commit_weight * offset_scale * squashed)
        * offset_scale
        * (1.0 - squashed * squashed)
        * scale
    )
    proj_part = dot(step, pooled, 1, 0, highest)
    pg_t = dot(proj_t, step, 0, 0, highest) * 0.25

    lane = lax.broadcasted_iota(jnp.int32, (C, W), 1)
    bias_sum = jnp.zeros((C, W), f32)
    for f in range(F):
        for h in range(R):
            g = pg_t[:, h * W : (h + 1) * W] * slope_t[f * R + h]
            bias_sum = bias_sum + g
            q0 = (f * R + h) * W
            gt[0:C, q0 : q0 + W] = jnp.where(lane == W - 1, 0.0, pltpu.roll(g, W - 1, 1)).astype(bf16)
            gt[C : 2 * C, q0 : q0 + W] = g.astype(bf16)
            gt[2 * C :, q0 : q0 + W] = jnp.where(lane == 0, 0.0, pltpu.roll(g, 1, 1)).astype(bf16)

    def small_plane(k):
        dx, ds = plane[k]
        return remote(
            sm_send, sm_recv.at[k], ss_s.at[k], ss_r.at[k],
            z * X + lax.rem(x + dx, X), lax.rem(s + ds, S),
        )

    def small_z(d):
        return remote(sz_send, sz_recv.at[d], sz_s.at[d], sz_r.at[d], lax.rem(z + d, Z) * X + x, s)


    def core_copy(g):
        lo, hi = units[g]
        return remote(
            acc.at[1 - core, lo:hi], recv1.at[lo:hi], core_s.at[g], core_r.at[g],
            t, s + 1 - 2 * core,
        )

    units = [(k, k + 3) for k in range(0, KC // G, 3)]
    spans = [(c, c + 1) for c in range(Z)]

    def plane_copy(c, dy, dx):
        ty, tx, k = lax.rem(y + dy, Y), lax.rem(x + dx, X), dy * X + dx
        lo, hi = spans[c]
        return remote(
            stage2.at[ty, tx, lo:hi], recv2.at[k, lo:hi], y_s.at[c, k], y_r.at[c, k],
            z * X + tx, ty * 2 + core,
        )

    def z_copy(to, slot):
        return remote(stage3.at[to], recv3.at[slot], tm_s.at[to], tm_r.at[slot], to * X + x, s)

    peers = [(dy, dx) for dy in range(Y) for dx in range(X) if dy or dx]
    chunks = sorted(range(Z), key=lambda c: -max(c, Z - 1 - c))

    def groups_of(c):
        return range(c * KZ // G, ((c + 1) * KZ - 1) // G + 1)

    order = []
    for c in chunks:
        order += [g for g in groups_of(c) if g not in order]
    sets = [order[k : k + 2] for k in range(0, len(order), 2)]

    done = set()

    def products(groups):
        done.update(groups)
        rhs = jnp.concatenate(
            [xb[g // 3 : g // 3 + F, g % 3 : g % 3 + R].reshape(F * cells, C) for g in groups], 1
        )
        res = dot(gt[...], rhs, 1, 0)
        for n, g in enumerate(groups):
            for c in range(3):
                for sp in range(S):
                    acc[sp % 2, g, sp // 2, :, c * C : (c + 1) * C] = res[
                        c * C + sp * oc : c * C + (sp + 1) * oc, n * C : (n + 1) * C
                    ]
        for u, (lo, hi) in enumerate(units):
            if any(lo <= g < hi for g in groups) and done.issuperset(range(lo, hi)):
                core_copy(u).start()

    half_lane = lax.broadcasted_iota(jnp.int32, (oc // 2, 128), 1) < 64
    arrived = set()

    def fold_core(c):
        for u, (lo, hi) in enumerate(units):
            if u not in arrived and any(lo <= g < hi for g in groups_of(c)):
                core_copy(u).wait_recv()
                arrived.add(u)
        for yy in range(Y):
            for xx in range(X):
                off = (c * X + xx) * KT
                base = off // 128 * 128
                wide = min(-(-KT // 128) * 128 + 128, KC - base)
                win = jnp.concatenate(
                    [
                        acc[core, k // 3, yy, :, k % 3 * C : (k % 3 + 1) * C]
                        + recv1[k // 3, yy, :, k % 3 * C : (k % 3 + 1) * C]
                        for k in range(base // C, (base + wide) // C)
                    ],
                    1,
                )
                if off > base:
                    win = pltpu.roll(win, wide - (off - base), 1)
                pieces = [win[:, 128 * k : 128 * (k + 1)] for k in range(full)]
                if rest:
                    last = win[:, 128 * full : 128 * (full + 1)]
                    if folded:
                        last = jnp.where(
                            half_lane, last[: oc // 2], pltpu.roll(last[oc // 2 :], 64, 1)
                        )
                    pieces.append(last)
                block = jnp.concatenate(pieces, 0)
                sum2[c, yy, xx] = block
                stage2[yy, xx, c] = block.astype(link_type)
        for k, (lo, hi) in enumerate(spans):
            if c == hi - 1:
                for dy, dx in peers:
                    plane_copy(k, dy, dx).start()

    def fold_plane(c):
        v = sum2[c, y, x]
        for k, (lo, hi) in enumerate(spans):
            if c == lo:
                for dy, dx in peers:
                    plane_copy(k, dy, dx).wait_recv()
        for dy, dx in peers:
            v = v + recv2[dy * X + dx, c].astype(f32)
        own3[c] = v
        stage3[c] = v.astype(link_type)
        start_if(z != c, z_copy(c, z))

    bias_part = dot(jnp.ones((8, W), f32), bias_sum, 1, 1, highest)
    sm_send[...] = jnp.where(lax.broadcasted_iota(jnp.int32, (8, C), 0) == L, bias_part, proj_part)
    for k in range(len(plane)):
        small_plane(k).start()

    ready = {}
    computed = []
    waiting = list(chunks)
    for n, groups in enumerate(sets):
        products(groups)
        if ready.get("next") is not None:
            fold_core(ready.pop("next"))
        computed += groups
        if waiting and all(g in computed for g in groups_of(waiting[0])):
            ready["next"] = waiting.pop(0)
    if ready.get("next") is not None:
        fold_core(ready.pop("next"))
    for c in waiting:
        fold_core(c)

    sm = sm_send[...]
    for k in range(len(plane)):
        small_plane(k).wait_recv()
        sm = sm + sm_recv[k]
    sz_send[...] = sm
    for d in range(1, Z):
        small_z(d).start()
    for c in chunks:
        fold_plane(c)
    for d in range(1, Z):
        small_z(d).wait_recv()
        sm = sm + sz_recv[d]
    small_out[...] = sm

    res = own3[z]
    for d in range(1, Z):
        src = lax.rem(z + d, Z)
        z_copy(src, src).wait_recv()
        res = res + recv3[src].astype(f32)
    for k in range(full):
        weight_out[:, 128 * k : 128 * (k + 1)] = res[k * oc : (k + 1) * oc]
    if rest:
        last = res[full * oc :]
        if folded:
            last = jnp.concatenate([last, pltpu.roll(last, 64, 1)], 0)
        weight_out[:, 128 * full :] = last[:, :rest]

    sent_if(up_s, row_up)
    sent_if(dn_s, row_dn)
    sent_if(up_t, inner)
    sent_if(late_dn, pass_dn)
    sent_if(late_up, pass_up)
    for d in range(1, X):
        cgx_copy(d).wait_send()
    for d in range(1, Z):
        cgz_copy(d).wait_send()
        small_z(d).wait_send()
    for k in range(len(plane)):
        small_plane(k).wait_send()
    for u in range(len(units)):
        core_copy(u).wait_send()
    for k in range(len(spans)):
        for dy, dx in peers:
            plane_copy(k, dy, dx).wait_send()
    for c in range(Z):
        sent_if(z != c, z_copy(c, z))


def finish_kernel(levels, centres, wg, small, quant_out, weight_out, proj_out, bias_out):
    L = levels.shape[0]
    lane = lax.broadcasted_iota(jnp.int32, centres.shape, 2)
    half = per_level(levels, lax.rem(lane, L), L)
    quant_out[...] = (centres[...].astype(f32) - half) / half
    weight_out[...] = wg[...]
    proj_out[...] = small[0:L]
    bias_out[...] = small[L : L + 1]


def on_device(T, S, frames, conv_weight, conv_bias, projection, levels, centres, code_grad):
    F, R, W, C = frames.shape
    KC = conv_weight.shape[0]
    KT = KC // T
    oc, Y, cells = C // S, S // 2, R * W
    Z, X = grid_of(T)
    PB = packed_rows(oc, KT)[3]
    L, TILE = levels.shape[0], code_grad.shape[2]
    scale = float(F * T * R * S * W) ** -0.5
    vmem = pl.BlockSpec(memory_space=pltpu.VMEM)
    dma = pltpu.SemaphoreType.DMA
    wg, small = pl.pallas_call(
        functools.partial(block_kernel, T, S, scale),
        out_shape=(
            pltpu.VMEM((oc, KT), f32),
            pltpu.VMEM((8, C), f32),
        ),
        in_specs=[pl.BlockSpec(memory_space=pl.ANY)] * 6,
        out_specs=(vmem, vmem),
        scratch_shapes=[
            pltpu.VMEM((F + 2, R + 2, W, C), bf16),
            pltpu.VMEM((KC, C), bf16),
            pltpu.VMEM((1, C), f32),
            pltpu.VMEM((L, C), f32),
            pltpu.SMEM((L,), jnp.int32),
            pltpu.VMEM((T, R, TILE), f32),
            pltpu.VMEM((Z, X, 8, 128), f32),
            pltpu.VMEM((X, Z, 8, 128), f32),
            pltpu.VMEM((Z, X, 8, 128), f32),
            pltpu.VMEM((8, C), f32),
            pltpu.VMEM((2, cells, 3 * C), f32),
            pltpu.VMEM((F * R, C, W), f32),
            pltpu.VMEM((3 * C, F * cells), bf16),
            pltpu.VMEM((2, 9, Y, oc, 3 * C), f32),
            pltpu.VMEM((9, Y, oc, 3 * C), f32),
            pltpu.VMEM((Z, Y, X, PB, 128), f32),
            pltpu.VMEM((Y, X, Z, PB, 128), link_type),
            pltpu.VMEM((Y * X, Z, PB, 128), link_type),
            pltpu.VMEM((Z, PB, 128), f32),
            pltpu.VMEM((Z, PB, 128), link_type),
            pltpu.VMEM((Z, PB, 128), link_type),
            pltpu.VMEM((8, C), f32),
            pltpu.VMEM((S * X, 8, C), f32),
            pltpu.VMEM((8, C), f32),
            pltpu.VMEM((Z, 8, C), f32),
            dma((8,)), pltpu.SemaphoreType.REGULAR((max(Z - 2, 1), 2)),
            dma((7,)), dma((7,)), dma((X,)), dma((X,)), dma((Z,)), dma((Z,)),
            dma((S * X,)), dma((S * X,)), dma((Z,)), dma((Z,)),
            dma((9,)), dma((9,)), dma((Z, Y * X)), dma((Z, Y * X)), dma((Z,)), dma((Z,)),
        ],
        compiler_params=pltpu.CompilerParams(
            collective_id=0, has_side_effects=True, vmem_limit_bytes=56 * 1024 * 1024
        ),
    )(frames, conv_weight, conv_bias.reshape(1, C), projection.T, levels, code_grad)
    quantized, wg, proj_grad, bias_grad = pl.pallas_call(
        finish_kernel,
        out_shape=(
            jax.ShapeDtypeStruct(centres.shape, f32),
            jax.ShapeDtypeStruct(wg.shape, f32),
            jax.ShapeDtypeStruct((L, C), f32),
            jax.ShapeDtypeStruct((1, C), f32),
        ),
        in_specs=[pl.BlockSpec(memory_space=pltpu.SMEM), vmem, vmem, vmem],
        out_specs=(vmem,) * 4,
    )(
        levels, centres,
        pltpu.with_memory_space_constraint(wg, pltpu.VMEM),
        pltpu.with_memory_space_constraint(small, pltpu.VMEM),
    )
    return quantized, wg.T, proj_grad.T, bias_grad.reshape(C)


def solution(mesh):
    return jax.shard_map(
        functools.partial(on_device, mesh.shape["tm"], mesh.shape["space"]),
        mesh=mesh,
        in_specs=(
            P("tm", "space", None, None),
            P(),
            P(),
            P(),
            P(),
            P(None, "space", "tm"),
            P(None, "space", "tm"),
        ),
        out_specs=(P(None, "space", "tm"), P("tm", "space"), P(), P()),
        check_vma=False,
    )
```

```python
import functools

import jax
import jax.numpy as jnp
from jax import lax
from jax.experimental import pallas as pl
from jax.experimental.pallas import tpu as pltpu
from jax.sharding import PartitionSpec as P

offset_scale = 0.45
commit_weight = 0.25
highest = lax.Precision.HIGHEST
MESH = pl.DeviceIdType.MESH
f32, bf16 = jnp.float32, jnp.bfloat16
link_type = bf16


def dot(a, b, ca, cb, precision=None):
    return lax.dot_general(
        a, b, (((ca,), (cb,)), ((), ())), preferred_element_type=f32, precision=precision
    )


def per_level(levels_ref, index, count):
    half = jnp.ones(index.shape, f32)
    for j in range(count):
        half = jnp.where(index == j, (levels_ref[j].astype(f32) - 1.0) * 0.5, half)
    return half


def grid_of(T):
    X = max(d for d in range(1, T + 1) if T % d == 0 and d * d <= T)
    return T // X, X


def packed_rows(oc, KT):
    full, rest = KT // 128, KT % 128
    folded = 0 < rest <= 64 and oc % 32 == 0
    return full, rest, folded, full * oc + (oc // 2 if folded else oc if rest else 0)


def block_kernel(
    T, S, scale,
    frames, weight_in, bias_in, proj_in, levels_in, code_in, centres_in,
    weight_out, small_out, quant_out,
    centres, xb, weight, bias, proj, levels, code_grad, cg_a, cg_b, cg_c, pscr, part, slope_t, gt, acc, recv1,
    sum2, stage2, recv2, own3, stage3, recv3,
    sm_send, sm_recv, sz_send, sz_recv,
    local_sem, token, halo_s, halo_r, cx_s, cx_r, cz_s, cz_r, ss_s, ss_r, sz_s, sz_r,
    core_s, core_r, y_s, y_r, tm_s, tm_r,
):
    Y = S // 2
    Z, X = grid_of(T)
    F, R, W, C = frames.shape
    L = levels_in.shape[0]
    TILE = code_in.shape[2]
    oc = C // S
    KC = weight_in.shape[0]
    KT = KC // T
    KZ = KT * X
    G = 3 * C
    full, rest, folded, PB = packed_rows(oc, KT)
    cells = R * W
    t = lax.axis_index("tm")
    s = lax.axis_index("space")
    y, core = s // 2, s % 2
    z, x = t // X, t % X
    up_t, dn_t, up_s, dn_s = t < T - 1, t > 0, s < S - 1, s > 0
    up_z, dn_z = z < Z - 1, z > 0
    turn_up = jnp.logical_and(up_t, x == X - 1)
    turn_dn = jnp.logical_and(dn_t, x == 0)

    barrier = pltpu.get_barrier_semaphore()

    def signal(tt, ss, sem=barrier):
        pl.semaphore_signal(sem, inc=1, device_id=(tt, ss), device_id_type=MESH)

    def signal_if(cond, tt, ss, sem=barrier):
        @pl.when(cond)
        def _():
            signal(tt, ss, sem)

    signal_if(turn_up, t + 1, s)
    signal_if(turn_dn, t - 1, s)
    signal_if(up_z, t + X, s)
    signal_if(dn_z, t - X, s)
    plane = [(dx, ds) for dx in range(X) for ds in range(S) if dx or ds]
    for dx, ds in plane:
        signal(z * X + lax.rem(x + dx, X), lax.rem(s + ds, S))

    own = pltpu.make_async_copy(frames, xb.at[2 : 2 + F, 1 : 1 + R], local_sem.at[0])
    first = [
        pltpu.make_async_copy(frames.at[0], xb.at[k, 1 : 1 + R], local_sem.at[1 + k])
        for k in range(2)
    ]
    code_load = pltpu.make_async_copy(code_in, code_grad, local_sem.at[3])
    proj_load = pltpu.make_async_copy(proj_in, proj, local_sem.at[4])
    bias_load = pltpu.make_async_copy(bias_in, bias, local_sem.at[5])
    levels_load = pltpu.make_async_copy(levels_in, levels, local_sem.at[6])
    weight_load = pltpu.make_async_copy(weight_in, weight, local_sem.at[7])
    centres_load = pltpu.make_async_copy(centres_in, centres, local_sem.at[8])
    code_load.start()
    own.start()
    weight_load.start()
    proj_load.start()
    bias_load.start()
    levels_load.start()
    centres_load.start()

    @pl.when(t == 0)
    def _():
        for copy in first:
            copy.start()

    cg_a[...] = jnp.zeros_like(cg_a)
    pscr[...] = jnp.zeros_like(pscr)

    @pl.when(s == 0)
    def _():
        xb[:, 0] = jnp.zeros((F + 2, W, C), bf16)

    @pl.when(s == S - 1)
    def _():
        xb[:, R + 1] = jnp.zeros((F + 2, W, C), bf16)

    code_load.wait()
    for k in range(T):
        cg_a[k // X, k % X, 0:R, 0:TILE] = code_grad[k]
    cg_b[0] = cg_a[:, x]

    one = lambda c: jnp.where(c, 1, 0)
    pl.semaphore_wait(
        barrier,
        (S * X - 1) + one(up_z) + one(dn_z) + one(turn_up) + one(turn_dn),
    )

    def remote(src, dst, ss_, rs_, tt, sp):
        return pltpu.make_async_remote_copy(
            src_ref=src, dst_ref=dst, send_sem=ss_, recv_sem=rs_,
            device_id=(tt, sp), device_id_type=MESH,
        )

    def start_if(cond, copy):
        @pl.when(cond)
        def _():
            copy.start()

    def recv_if(cond, copy):
        @pl.when(cond)
        def _():
            copy.wait_recv()

    def sent_if(cond, copy):
        @pl.when(cond)
        def _():
            copy.wait_send()

    def cgx_copy(d):
        to = lax.rem(x + d, X)
        return remote(cg_a.at[:, to], cg_b.at[d], cx_s.at[d], cx_r.at[d], z * X + to, s)

    def cgz_copy(d):
        to = lax.rem(z + d, Z)
        return remote(cg_b.at[:, to], cg_c.at[d], cz_s.at[d], cz_r.at[d], to * X + x, s)

    H = R + 1

    def halo(k, src, dst, tt, sp):
        return remote(src, dst, halo_s.at[k], halo_r.at[k], tt, sp)

    row_up = halo(0, frames.at[:, R - 1], xb.at[2 : 2 + F, 0], t, s + 1)
    row_dn = halo(1, frames.at[:, 0], xb.at[2 : 2 + F, H], t, s - 1)
    edge_lo = halo(2, frames.at[F - 2 : F, 0], xb.at[0:2, 1], t + 1, s)
    edge_hi = halo(3, frames.at[F - 2 : F, R - 1], xb.at[0:2, R], t + 1, s)
    inner = halo(4, frames.at[F - 2 : F, 1 : R - 1], xb.at[0:2, 2:R], t + 1, s)
    pass_dn = halo(5, xb.at[0:2, 1], xb.at[0:2, H], t, s - 1)
    pass_up = halo(6, xb.at[0:2, R], xb.at[0:2, 0], t, s + 1)
    late_dn, late_up = jnp.logical_and(dn_t, dn_s), jnp.logical_and(dn_t, up_s)

    rounds = max(Z - 2, 0)

    def chain(side):
        sends, gets, to = ((up_z, dn_z, t + X), (dn_z, up_z, t - X))[side]
        for r in range(rounds):
            @pl.when(gets)
            def _():
                pl.semaphore_wait(token.at[r, side], 1)

            if r + 1 < rounds:
                signal_if(sends, to, s, token.at[r + 1, side])

    def cgz_start(upper):
        for d in range(1, Z):
            above = lax.rem(z + d, Z) > z
            start_if(above if upper else jnp.logical_not(above), cgz_copy(d))

    if rounds:
        signal_if(up_z, t + X, s, token.at[0, 0])
        signal_if(dn_z, t - X, s, token.at[0, 1])
    for d in range(1, X):
        cgx_copy(d).start()
    start_if(up_t, edge_lo)
    start_if(up_t, edge_hi)
    start_if(up_s, row_up)
    start_if(dn_s, row_dn)
    sent_if(up_t, edge_lo)
    sent_if(up_t, edge_hi)
    start_if(up_t, inner)
    proj_load.wait()
    bias_load.wait()
    levels_load.wait()
    centres_load.wait()
    column = lax.broadcasted_iota(jnp.int32, centres.shape, 2)
    half = per_level(levels, lax.rem(column, L), L)
    quant_out[...] = (centres[...].astype(f32) - half) / half
    pscr[0:L] = proj[...]
    proj_t = pscr[...]
    row = lax.broadcasted_iota(jnp.int32, (cells, C), 0) % W

    def taps(f, times):
        slabs = []
        weights = []
        for a in times:
            for b in range(3):
                slabs.append(xb[f + a, b : b + R].reshape(cells, C))
                k0 = (a * 3 + b) * G
                weights.append(
                    jnp.concatenate([weight[k0 + c * C : k0 + (c + 1) * C] for c in range(3)], 1)
                )
        return dot(jnp.concatenate(slabs, 1), jnp.concatenate(weights, 0), 1, 0)

    def frame_end(f, out):
        left = jnp.where(row == 0, 0.0, pltpu.roll(out[:, 0:C], 1, 0))
        right = jnp.where(row == W - 1, 0.0, pltpu.roll(out[:, 2 * C :], cells - 1, 0))
        pre = out[:, C : 2 * C] + bias[...] + left + right
        sig = 1.0 / (1.0 + jnp.exp(-pre))
        act = (pre * sig).astype(bf16).astype(f32)
        slope = sig * (1.0 + pre * (1.0 - sig))
        for h in range(R):
            slope_t[f * R + h] = slope[h * W : (h + 1) * W].T
        return act

    own.wait()
    weight_load.wait()
    recv_if(dn_s, row_up)
    recv_if(up_s, row_dn)
    pooled = frame_end(2, taps(2, (0, 1, 2)))

    chain(0)
    for d in range(1, X):
        cgx_copy(d).wait_recv()
    cgz_start(False)
    chain(1)
    cgz_start(True)
    recv_if(dn_t, edge_lo)
    start_if(late_dn, pass_dn)
    recv_if(dn_t, edge_hi)
    start_if(late_up, pass_up)
    pooled = pooled + frame_end(3, taps(3, (0, 1, 2)))
    part[0] = taps(0, (2,))
    part[1] = taps(1, (1, 2))

    @pl.when(t == 0)
    def _():
        for k in range(2):
            first[k].wait()
            xb[k, 0] = xb[2, 0]
            xb[k, H] = xb[2, H]

    recv_if(dn_t, inner)
    recv_if(late_up, pass_dn)
    recv_if(late_dn, pass_up)
    pooled = pooled + frame_end(0, part[0] + taps(0, (0, 1)))
    pooled = (pooled + frame_end(1, part[1] + taps(1, (0,)))) * 0.25

    latent = dot(proj_t, pooled, 1, 1, highest)
    cg_c[0] = cg_b[:, z]
    for d in range(1, Z):
        cgz_copy(d).wait_recv()
    wt = TILE // L
    cg_all = cg_c[...].reshape(T * 8, 128)
    r_i = lax.broadcasted_iota(jnp.int32, (T * 8, cells), 0)
    q_i = lax.broadcasted_iota(jnp.int32, (T * 8, cells), 1)
    piece = r_i // 8
    owner = lax.rem(z - piece // X + Z, Z) * X + lax.rem(x - piece % X + X, X)
    pick = jnp.logical_and(r_i % 8 == q_i // W, owner == (q_i % W) // wt).astype(f32)
    spread = dot(cg_all, pick, 0, 0, highest)
    l_i = lax.broadcasted_iota(jnp.int32, (128, cells), 0)
    w_i = lax.broadcasted_iota(jnp.int32, (128, cells), 1) % W
    spread = jnp.where(jnp.logical_and(l_i // L == w_i % wt, l_i < TILE), spread, 0.0)
    j_i = lax.broadcasted_iota(jnp.int32, (8, 128), 0)
    m_i = lax.broadcasted_iota(jnp.int32, (8, 128), 1)
    fold = jnp.logical_and(m_i % L == j_i, m_i < TILE).astype(f32)
    code = dot(fold, spread, 1, 0, highest)
    half_j = per_level(levels, lax.broadcasted_iota(jnp.int32, (8, cells), 0), L)
    code = code / half_j

    squashed = jnp.tanh(latent)
    step = (
        (code + 2.0 * commit_weight * offset_scale * squashed)
        * offset_scale
        * (1.0 - squashed * squashed)
        * scale
    )
    proj_part = dot(step, pooled, 1, 0, highest)
    pg_t = dot(proj_t, step, 0, 0, highest) * 0.25

    lane = lax.broadcasted_iota(jnp.int32, (C, W), 1)
    bias_sum = jnp.zeros((C, W), f32)
    for f in range(F):
        for h in range(R):
            g = pg_t[:, h * W : (h + 1) * W] * slope_t[f * R + h]
            bias_sum = bias_sum + g
            q0 = (f * R + h) * W
            gt[0:C, q0 : q0 + W] = jnp.where(lane == W - 1, 0.0, pltpu.roll(g, W - 1, 1)).astype(bf16)
            gt[C : 2 * C, q0 : q0 + W] = g.astype(bf16)
            gt[2 * C :, q0 : q0 + W] = jnp.where(lane == 0, 0.0, pltpu.roll(g, 1, 1)).astype(bf16)

    def small_plane(k):
        dx, ds = plane[k]
        return remote(
            sm_send, sm_recv.at[k], ss_s.at[k], ss_r.at[k],
            z * X + lax.rem(x + dx, X), lax.rem(s + ds, S),
        )

    def small_z(d):
        return remote(sz_send, sz_recv.at[d], sz_s.at[d], sz_r.at[d], lax.rem(z + d, Z) * X + x, s)


    def core_copy(g):
        lo, hi = units[g]
        return remote(
            acc.at[1 - core, lo:hi], recv1.at[lo:hi], core_s.at[g], core_r.at[g],
            t, s + 1 - 2 * core,
        )

    def groups_of(c):
        return range(c * KZ // G, ((c + 1) * KZ - 1) // G + 1)

    chunks = sorted(range(Z), key=lambda c: -max(c, Z - 1 - c))
    order, units = [], []
    for c in chunks:
        fresh = [g for g in groups_of(c) if g not in order]
        order += fresh
        if fresh:
            units.append((fresh[0], fresh[-1] + 1))
    sets = [order[k : k + 2] for k in range(0, len(order), 2)]

    spans = [(c, c + 1) for c in range(Z)]

    def plane_copy(c, dy, dx):
        ty, tx, k = lax.rem(y + dy, Y), lax.rem(x + dx, X), dy * X + dx
        lo, hi = spans[c]
        return remote(
            stage2.at[ty, tx, lo:hi], recv2.at[k, lo:hi], y_s.at[c, k], y_r.at[c, k],
            z * X + tx, ty * 2 + core,
        )

    def z_copy(to, slot):
        return remote(stage3.at[to], recv3.at[slot], tm_s.at[to], tm_r.at[slot], to * X + x, s)

    peers = [(dy, dx) for dy in range(Y) for dx in range(X) if dy or dx]
    def products(groups):
        rhs = jnp.concatenate(
            [xb[g // 3 : g // 3 + F, g % 3 : g % 3 + R].reshape(F * cells, C) for g in groups], 1
        )
        res = dot(gt[...], rhs, 1, 0)
        for n, g in enumerate(groups):
            for c in range(3):
                for sp in range(S):
                    acc[sp % 2, g, sp // 2, :, c * C : (c + 1) * C] = res[
                        c * C + sp * oc : c * C + (sp + 1) * oc, n * C : (n + 1) * C
                    ]
        for u, (lo, hi) in enumerate(units):
            if max(order.index(g) for g in range(lo, hi)) in [order.index(g) for g in groups]:
                core_copy(u).start()

    half_lane = lax.broadcasted_iota(jnp.int32, (oc // 2, 128), 1) < 64
    arrived = set()

    def fold_core(c):
        for u, (lo, hi) in enumerate(units):
            if u not in arrived and any(lo <= g < hi for g in groups_of(c)):
                core_copy(u).wait_recv()
                arrived.add(u)
        for yy in range(Y):
            for xx in range(X):
                off = (c * X + xx) * KT
                base = off // 128 * 128
                wide = min(-(-KT // 128) * 128 + 128, KC - base)
                win = jnp.concatenate(
                    [
                        acc[core, k // 3, yy, :, k % 3 * C : (k % 3 + 1) * C]
                        + recv1[k // 3, yy, :, k % 3 * C : (k % 3 + 1) * C]
                        for k in range(base // C, (base + wide) // C)
                    ],
                    1,
                )
                if off > base:
                    win = pltpu.roll(win, wide - (off - base), 1)
                pieces = [win[:, 128 * k : 128 * (k + 1)] for k in range(full)]
                if rest:
                    last = win[:, 128 * full : 128 * (full + 1)]
                    if folded:
                        last = jnp.where(
                            half_lane, last[: oc // 2], pltpu.roll(last[oc // 2 :], 64, 1)
                        )
                    pieces.append(last)
                block = jnp.concatenate(pieces, 0)
                sum2[c, yy, xx] = block
                stage2[yy, xx, c] = block.astype(link_type)
        for k, (lo, hi) in enumerate(spans):
            if c == hi - 1:
                for dy, dx in peers:
                    plane_copy(k, dy, dx).start()

    def fold_plane(c):
        v = sum2[c, y, x]
        for k, (lo, hi) in enumerate(spans):
            if c == lo:
                for dy, dx in peers:
                    plane_copy(k, dy, dx).wait_recv()
        for dy, dx in peers:
            v = v + recv2[dy * X + dx, c].astype(f32)
        own3[c] = v
        stage3[c] = v.astype(link_type)
        start_if(z != c, z_copy(c, z))

    bias_part = dot(jnp.ones((8, W), f32), bias_sum, 1, 1, highest)
    sm_send[...] = jnp.where(lax.broadcasted_iota(jnp.int32, (8, C), 0) == L, bias_part, proj_part)
    for k in range(len(plane)):
        small_plane(k).start()

    waiting = list(chunks)
    for n, groups in enumerate(sets):
        products(groups)
        known = sum((sets[k] for k in range(n + 1 - 1)), [])
        while waiting and all(g in known for g in groups_of(waiting[0])):
            fold_core(waiting.pop(0))
    for c in waiting:
        fold_core(c)

    sm = sm_send[...]
    for k in range(len(plane)):
        small_plane(k).wait_recv()
        sm = sm + sm_recv[k]
    sz_send[...] = sm
    for d in range(1, Z):
        small_z(d).start()
    for c in chunks:
        fold_plane(c)
    for d in range(1, Z):
        small_z(d).wait_recv()
        sm = sm + sz_recv[d]
    small_out[...] = sm

    res = own3[z]
    for d in range(1, Z):
        src = lax.rem(z + d, Z)
        z_copy(src, src).wait_recv()
        res = res + recv3[src].astype(f32)
    for k in range(full):
        weight_out[:, 128 * k : 128 * (k + 1)] = res[k * oc : (k + 1) * oc]
    if rest:
        last = res[full * oc :]
        if folded:
            last = jnp.concatenate([last, pltpu.roll(last, 64, 1)], 0)
        weight_out[:, 128 * full :] = last[:, :rest]

    sent_if(up_s, row_up)
    sent_if(dn_s, row_dn)
    sent_if(up_t, inner)
    sent_if(late_dn, pass_dn)
    sent_if(late_up, pass_up)
    for d in range(1, X):
        cgx_copy(d).wait_send()
    for d in range(1, Z):
        cgz_copy(d).wait_send()
        small_z(d).wait_send()
    for k in range(len(plane)):
        small_plane(k).wait_send()
    for u in range(len(units)):
        core_copy(u).wait_send()
    for k in range(len(spans)):
        for dy, dx in peers:
            plane_copy(k, dy, dx).wait_send()
    for c in range(Z):
        sent_if(z != c, z_copy(c, z))


def finish_kernel(quant, wg, small, quant_out, weight_out, proj_out, bias_out):
    L = proj_out.shape[0]
    quant_out[...] = quant[...]
    weight_out[...] = wg[...]
    proj_out[...] = small[0:L]
    bias_out[...] = small[L : L + 1]


def on_device(T, S, frames, conv_weight, conv_bias, projection, levels, centres, code_grad):
    F, R, W, C = frames.shape
    KC = conv_weight.shape[0]
    KT = KC // T
    oc, Y, cells = C // S, S // 2, R * W
    Z, X = grid_of(T)
    PB = packed_rows(oc, KT)[3]
    L, TILE = levels.shape[0], code_grad.shape[2]
    scale = float(F * T * R * S * W) ** -0.5
    vmem = pl.BlockSpec(memory_space=pltpu.VMEM)
    dma = pltpu.SemaphoreType.DMA
    held = pl.pallas_call(
        functools.partial(block_kernel, T, S, scale),
        out_shape=(
            pltpu.VMEM((oc, KT), f32),
            pltpu.VMEM((8, C), f32),
            pltpu.VMEM(centres.shape, f32),
        ),
        in_specs=[pl.BlockSpec(memory_space=pl.ANY)] * 7,
        out_specs=(vmem,) * 3,
        scratch_shapes=[
            pltpu.VMEM(centres.shape, jnp.int32),
            pltpu.VMEM((F + 2, R + 2, W, C), bf16),
            pltpu.VMEM((KC, C), bf16),
            pltpu.VMEM((1, C), f32),
            pltpu.VMEM((L, C), f32),
            pltpu.SMEM((L,), jnp.int32),
            pltpu.VMEM((T, R, TILE), f32),
            pltpu.VMEM((Z, X, 8, 128), f32),
            pltpu.VMEM((X, Z, 8, 128), f32),
            pltpu.VMEM((Z, X, 8, 128), f32),
            pltpu.VMEM((8, C), f32),
            pltpu.VMEM((2, cells, 3 * C), f32),
            pltpu.VMEM((F * R, C, W), f32),
            pltpu.VMEM((3 * C, F * cells), bf16),
            pltpu.VMEM((2, 9, Y, oc, 3 * C), f32),
            pltpu.VMEM((9, Y, oc, 3 * C), f32),
            pltpu.VMEM((Z, Y, X, PB, 128), f32),
            pltpu.VMEM((Y, X, Z, PB, 128), link_type),
            pltpu.VMEM((Y * X, Z, PB, 128), link_type),
            pltpu.VMEM((Z, PB, 128), f32),
            pltpu.VMEM((Z, PB, 128), link_type),
            pltpu.VMEM((Z, PB, 128), link_type),
            pltpu.VMEM((8, C), f32),
            pltpu.VMEM((S * X, 8, C), f32),
            pltpu.VMEM((8, C), f32),
            pltpu.VMEM((Z, 8, C), f32),
            dma((9,)), pltpu.SemaphoreType.REGULAR((max(Z - 2, 1), 2)),
            dma((7,)), dma((7,)), dma((X,)), dma((X,)), dma((Z,)), dma((Z,)),
            dma((S * X,)), dma((S * X,)), dma((Z,)), dma((Z,)),
            dma((9,)), dma((9,)), dma((Z, Y * X)), dma((Z, Y * X)), dma((Z,)), dma((Z,)),
        ],
        compiler_params=pltpu.CompilerParams(
            collective_id=0, has_side_effects=True, vmem_limit_bytes=56 * 1024 * 1024
        ),
    )(frames, conv_weight, conv_bias.reshape(1, C), projection.T, levels, code_grad, centres)
    wg, small, quantized = (
        pltpu.with_memory_space_constraint(v, pltpu.VMEM) for v in held
    )
    quantized, wg, proj_grad, bias_grad = pl.pallas_call(
        finish_kernel,
        out_shape=(
            jax.ShapeDtypeStruct(centres.shape, f32),
            jax.ShapeDtypeStruct(wg.shape, f32),
            jax.ShapeDtypeStruct((L, C), f32),
            jax.ShapeDtypeStruct((1, C), f32),
        ),
        in_specs=[vmem] * 3,
        out_specs=(vmem,) * 4,
    )(quantized, wg, small)
    return quantized, wg.T, proj_grad.T, bias_grad.reshape(C)


def solution(mesh):
    return jax.shard_map(
        functools.partial(on_device, mesh.shape["tm"], mesh.shape["space"]),
        mesh=mesh,
        in_specs=(
            P("tm", "space", None, None),
            P(),
            P(),
            P(),
            P(),
            P(None, "space", "tm"),
            P(None, "space", "tm"),
        ),
        out_specs=(P(None, "space", "tm"), P("tm", "space"), P(), P()),
        check_vma=False,
    )
```

```python
import functools

import jax
import jax.numpy as jnp
from jax import lax
from jax.experimental import pallas as pl
from jax.experimental.pallas import tpu as pltpu
from jax.sharding import PartitionSpec as P

offset_scale = 0.45
commit_weight = 0.25
highest = lax.Precision.HIGHEST
MESH = pl.DeviceIdType.MESH
f32, bf16 = jnp.float32, jnp.bfloat16
link_type = bf16


def dot(a, b, ca, cb, precision=None):
    return lax.dot_general(
        a, b, (((ca,), (cb,)), ((), ())), preferred_element_type=f32, precision=precision
    )


def per_level(levels_ref, index, count):
    half = jnp.ones(index.shape, f32)
    for j in range(count):
        half = jnp.where(index == j, (levels_ref[j].astype(f32) - 1.0) * 0.5, half)
    return half


def grid_of(T):
    X = max(d for d in range(1, T + 1) if T % d == 0 and d * d <= T)
    return T // X, X


def packed_rows(oc, KT):
    full, rest = KT // 128, KT % 128
    folded = 0 < rest <= 64 and oc % 32 == 0
    return full, rest, folded, full * oc + (oc // 2 if folded else oc if rest else 0)


def block_kernel(
    T, S, scale,
    frames, weight_in, bias_in, proj_in, levels_in, code_in, centres_in,
    weight_out, small_out, quant_out,
    centres, xb, weight, bias, proj, levels, code_grad, cg_a, cg_b, cg_c, pscr, part, slope_t, gt, acc, recv1,
    sum2, stage2, recv2, own3, stage3, recv3,
    sm_send, sm_recv, sz_send, sz_recv,
    local_sem, token, halo_s, halo_r, cx_s, cx_r, cz_s, cz_r, ss_s, ss_r, sz_s, sz_r,
    core_s, core_r, y_s, y_r, tm_s, tm_r,
):
    Y = S // 2
    Z, X = grid_of(T)
    F, R, W, C = frames.shape
    L = levels_in.shape[0]
    TILE = code_in.shape[2]
    oc = C // S
    KC = weight_in.shape[0]
    KT = KC // T
    KZ = KT * X
    G = 3 * C
    full, rest, folded, PB = packed_rows(oc, KT)
    cells = R * W
    t = lax.axis_index("tm")
    s = lax.axis_index("space")
    y, core = s // 2, s % 2
    z, x = t // X, t % X
    up_t, dn_t, up_s, dn_s = t < T - 1, t > 0, s < S - 1, s > 0
    up_z, dn_z = z < Z - 1, z > 0
    turn_up = jnp.logical_and(up_t, x == X - 1)
    turn_dn = jnp.logical_and(dn_t, x == 0)

    barrier = pltpu.get_barrier_semaphore()

    def signal(tt, ss, sem=barrier):
        pl.semaphore_signal(sem, inc=1, device_id=(tt, ss), device_id_type=MESH)

    def signal_if(cond, tt, ss, sem=barrier):
        @pl.when(cond)
        def _():
            signal(tt, ss, sem)

    signal_if(turn_up, t + 1, s)
    signal_if(turn_dn, t - 1, s)
    signal_if(up_z, t + X, s)
    signal_if(dn_z, t - X, s)
    plane = [(dx, ds) for dx in range(X) for ds in range(S) if dx or ds]
    for dx, ds in plane:
        signal(z * X + lax.rem(x + dx, X), lax.rem(s + ds, S))

    own = pltpu.make_async_copy(frames, xb.at[2 : 2 + F, 1 : 1 + R], local_sem.at[0])
    first = [
        pltpu.make_async_copy(frames.at[0], xb.at[k, 1 : 1 + R], local_sem.at[1 + k])
        for k in range(2)
    ]
    code_load = pltpu.make_async_copy(code_in, code_grad, local_sem.at[3])
    proj_load = pltpu.make_async_copy(proj_in, proj, local_sem.at[4])
    bias_load = pltpu.make_async_copy(bias_in, bias, local_sem.at[5])
    levels_load = pltpu.make_async_copy(levels_in, levels, local_sem.at[6])
    weight_load = pltpu.make_async_copy(weight_in, weight, local_sem.at[7])
    centres_load = pltpu.make_async_copy(centres_in, centres, local_sem.at[8])
    code_load.start()
    own.start()
    weight_load.start()
    proj_load.start()
    bias_load.start()
    levels_load.start()
    centres_load.start()

    @pl.when(t == 0)
    def _():
        for copy in first:
            copy.start()

    cg_a[...] = jnp.zeros_like(cg_a)
    pscr[...] = jnp.zeros_like(pscr)

    @pl.when(s == 0)
    def _():
        xb[:, 0] = jnp.zeros((F + 2, W, C), bf16)

    @pl.when(s == S - 1)
    def _():
        xb[:, R + 1] = jnp.zeros((F + 2, W, C), bf16)

    code_load.wait()
    for k in range(T):
        cg_a[k // X, k % X, 0:R, 0:TILE] = code_grad[k]
    cg_b[0] = cg_a[:, x]

    one = lambda c: jnp.where(c, 1, 0)
    pl.semaphore_wait(
        barrier,
        (S * X - 1) + one(up_z) + one(dn_z) + one(turn_up) + one(turn_dn),
    )

    def remote(src, dst, ss_, rs_, tt, sp):
        return pltpu.make_async_remote_copy(
            src_ref=src, dst_ref=dst, send_sem=ss_, recv_sem=rs_,
            device_id=(tt, sp), device_id_type=MESH,
        )

    def start_if(cond, copy):
        @pl.when(cond)
        def _():
            copy.start()

    def recv_if(cond, copy):
        @pl.when(cond)
        def _():
            copy.wait_recv()

    def sent_if(cond, copy):
        @pl.when(cond)
        def _():
            copy.wait_send()

    def cgx_copy(d):
        to = lax.rem(x + d, X)
        return remote(cg_a.at[:, to], cg_b.at[d], cx_s.at[d], cx_r.at[d], z * X + to, s)

    def cgz_copy(d):
        to = lax.rem(z + d, Z)
        return remote(cg_b.at[:, to], cg_c.at[d], cz_s.at[d], cz_r.at[d], to * X + x, s)

    H = R + 1

    def halo(k, src, dst, tt, sp):
        return remote(src, dst, halo_s.at[k], halo_r.at[k], tt, sp)

    row_up = halo(0, frames.at[:, R - 1], xb.at[2 : 2 + F, 0], t, s + 1)
    row_dn = halo(1, frames.at[:, 0], xb.at[2 : 2 + F, H], t, s - 1)
    edge_lo = halo(2, frames.at[F - 2 : F, 0], xb.at[0:2, 1], t + 1, s)
    edge_hi = halo(3, frames.at[F - 2 : F, R - 1], xb.at[0:2, R], t + 1, s)
    inner = halo(4, frames.at[F - 2 : F, 1 : R - 1], xb.at[0:2, 2:R], t + 1, s)
    pass_dn = halo(5, xb.at[0:2, 1], xb.at[0:2, H], t, s - 1)
    pass_up = halo(6, xb.at[0:2, R], xb.at[0:2, 0], t, s + 1)
    late_dn, late_up = jnp.logical_and(dn_t, dn_s), jnp.logical_and(dn_t, up_s)

    rounds = max(Z - 2, 0)

    def chain(side):
        sends, gets, to = ((up_z, dn_z, t + X), (dn_z, up_z, t - X))[side]
        for r in range(rounds):
            @pl.when(gets)
            def _():
                pl.semaphore_wait(token.at[r, side], 1)

            if r + 1 < rounds:
                signal_if(sends, to, s, token.at[r + 1, side])

    def cgz_start(upper):
        for d in range(1, Z):
            above = lax.rem(z + d, Z) > z
            start_if(above if upper else jnp.logical_not(above), cgz_copy(d))

    if rounds:
        signal_if(up_z, t + X, s, token.at[0, 0])
        signal_if(dn_z, t - X, s, token.at[0, 1])
    for d in range(1, X):
        cgx_copy(d).start()
    start_if(up_t, edge_lo)
    start_if(up_t, edge_hi)
    start_if(up_s, row_up)
    start_if(dn_s, row_dn)
    proj_load.wait()
    bias_load.wait()
    levels_load.wait()
    centres_load.wait()
    column = lax.broadcasted_iota(jnp.int32, centres.shape, 2)
    half = per_level(levels, lax.rem(column, L), L)
    quant_out[...] = (centres[...].astype(f32) - half) / half
    pscr[0:L] = proj[...]
    proj_t = pscr[...]
    def taps(jobs, times):
        slabs = []
        weights = []
        for a in times:
            for b in range(3):
                slabs.append(
                    jnp.concatenate(
                        [xb[f + a, lo + b : hi + b].reshape((hi - lo) * W, C) for f, lo, hi in jobs], 0
                    )
                )
                k0 = (a * 3 + b) * G
                weights.append(
                    jnp.concatenate([weight[k0 + c * C : k0 + (c + 1) * C] for c in range(3)], 1)
                )
        return dot(jnp.concatenate(slabs, 1), jnp.concatenate(weights, 0), 1, 0)

    sums = {}

    def rows_end(out, jobs):
        size = out.shape[0]
        row = lax.broadcasted_iota(jnp.int32, (size, C), 0) % W
        left = jnp.where(row == 0, 0.0, pltpu.roll(out[:, 0:C], 1, 0))
        right = jnp.where(row == W - 1, 0.0, pltpu.roll(out[:, 2 * C :], size - 1, 0))
        pre = out[:, C : 2 * C] + bias[...] + left + right
        sig = 1.0 / (1.0 + jnp.exp(-pre))
        act = (pre * sig).astype(bf16).astype(f32)
        slope = sig * (1.0 + pre * (1.0 - sig))
        lines = [(f, h) for f, lo, hi in jobs for h in range(lo, hi)]
        for n, (f, h) in enumerate(lines):
            slope_t[f * R + h] = slope[n * W : (n + 1) * W].T
            line = act[n * W : (n + 1) * W]
            sums[h] = sums[h] + line if h in sums else line

    inside = lambda f: [(f, 1, R - 1)]
    outside = lambda f: [(f, 0, 1), (f, R - 1, R)]

    def own_taps(place):
        for k, times in ((0, (2,)), (1, (1, 2))):
            out = taps(place(k), times)
            at = 0
            for _, lo, hi in place(k):
                part[k, lo * W : hi * W] = out[at : at + (hi - lo) * W]
                at += (hi - lo) * W

    def frames_of(place):
        return sum((place(f) for f in range(2, F)), [])

    own.wait()
    weight_load.wait()
    rows_end(taps(frames_of(inside), (0, 1, 2)), frames_of(inside))
    own_taps(inside)
    sent_if(up_t, edge_lo)
    sent_if(up_t, edge_hi)
    start_if(up_t, inner)
    recv_if(dn_s, row_up)
    recv_if(up_s, row_dn)
    rows_end(taps(frames_of(outside), (0, 1, 2)), frames_of(outside))
    recv_if(dn_t, edge_lo)
    start_if(late_dn, pass_dn)
    recv_if(dn_t, edge_hi)
    start_if(late_up, pass_up)
    chain(0)
    for d in range(1, X):
        cgx_copy(d).wait_recv()
    cgz_start(False)
    chain(1)
    cgz_start(True)
    own_taps(outside)

    @pl.when(t == 0)
    def _():
        for k in range(2):
            first[k].wait()
            xb[k, 0] = xb[2, 0]
            xb[k, H] = xb[2, H]

    recv_if(dn_t, inner)
    recv_if(late_up, pass_dn)
    recv_if(late_dn, pass_up)
    rows_end(part[0] + taps([(0, 0, R)], (0, 1)), [(0, 0, R)])
    rows_end(part[1] + taps([(1, 0, R)], (0,)), [(1, 0, R)])
    pooled = jnp.concatenate([sums[h] for h in range(R)], 0) * 0.25

    latent = dot(proj_t, pooled, 1, 1, highest)
    cg_c[0] = cg_b[:, z]
    for d in range(1, Z):
        cgz_copy(d).wait_recv()
    wt = TILE // L
    cg_all = cg_c[...].reshape(T * 8, 128)
    r_i = lax.broadcasted_iota(jnp.int32, (T * 8, cells), 0)
    q_i = lax.broadcasted_iota(jnp.int32, (T * 8, cells), 1)
    piece = r_i // 8
    owner = lax.rem(z - piece // X + Z, Z) * X + lax.rem(x - piece % X + X, X)
    pick = jnp.logical_and(r_i % 8 == q_i // W, owner == (q_i % W) // wt).astype(f32)
    spread = dot(cg_all, pick, 0, 0, highest)
    l_i = lax.broadcasted_iota(jnp.int32, (128, cells), 0)
    w_i = lax.broadcasted_iota(jnp.int32, (128, cells), 1) % W
    spread = jnp.where(jnp.logical_and(l_i // L == w_i % wt, l_i < TILE), spread, 0.0)
    j_i = lax.broadcasted_iota(jnp.int32, (8, 128), 0)
    m_i = lax.broadcasted_iota(jnp.int32, (8, 128), 1)
    fold = jnp.logical_and(m_i % L == j_i, m_i < TILE).astype(f32)
    code = dot(fold, spread, 1, 0, highest)
    half_j = per_level(levels, lax.broadcasted_iota(jnp.int32, (8, cells), 0), L)
    code = code / half_j

    squashed = jnp.tanh(latent)
    step = (
        (code + 2.0 * commit_weight * offset_scale * squashed)
        * offset_scale
        * (1.0 - squashed * squashed)
        * scale
    )
    pg_t = dot(proj_t, step, 0, 0, highest) * 0.25

    lane = lax.broadcasted_iota(jnp.int32, (C, W), 1)
    bias_sum = jnp.zeros((C, W), f32)
    for f in range(F):
        for h in range(R):
            g = pg_t[:, h * W : (h + 1) * W] * slope_t[f * R + h]
            bias_sum = bias_sum + g
            q0 = (f * R + h) * W
            gt[0:C, q0 : q0 + W] = jnp.where(lane == W - 1, 0.0, pltpu.roll(g, W - 1, 1)).astype(bf16)
            gt[C : 2 * C, q0 : q0 + W] = g.astype(bf16)
            gt[2 * C :, q0 : q0 + W] = jnp.where(lane == 0, 0.0, pltpu.roll(g, 1, 1)).astype(bf16)

    def small_plane(k):
        dx, ds = plane[k]
        return remote(
            sm_send, sm_recv.at[k], ss_s.at[k], ss_r.at[k],
            z * X + lax.rem(x + dx, X), lax.rem(s + ds, S),
        )

    def small_z(d):
        return remote(sz_send, sz_recv.at[d], sz_s.at[d], sz_r.at[d], lax.rem(z + d, Z) * X + x, s)


    def core_copy(g):
        lo, hi = units[g]
        return remote(
            acc.at[1 - core, lo:hi], recv1.at[lo:hi], core_s.at[g], core_r.at[g],
            t, s + 1 - 2 * core,
        )

    def groups_of(c):
        return range(c * KZ // G, ((c + 1) * KZ - 1) // G + 1)

    chunks = sorted(range(Z), key=lambda c: -max(c, Z - 1 - c))
    order, units = [], []
    for c in chunks:
        fresh = [g for g in groups_of(c) if g not in order]
        order += fresh
        if fresh:
            units.append((fresh[0], fresh[-1] + 1))
    sets = [order[k : k + 2] for k in range(0, len(order), 2)]

    spans = [(c, c + 1) for c in range(Z)]

    def plane_copy(c, dy, dx):
        ty, tx, k = lax.rem(y + dy, Y), lax.rem(x + dx, X), dy * X + dx
        lo, hi = spans[c]
        return remote(
            stage2.at[ty, tx, lo:hi], recv2.at[k, lo:hi], y_s.at[c, k], y_r.at[c, k],
            z * X + tx, ty * 2 + core,
        )

    def z_copy(to, slot):
        return remote(stage3.at[to], recv3.at[slot], tm_s.at[to], tm_r.at[slot], to * X + x, s)

    peers = [(dy, dx) for dy in range(Y) for dx in range(X) if dy or dx]
    def products(groups):
        rhs = jnp.concatenate(
            [xb[g // 3 : g // 3 + F, g % 3 : g % 3 + R].reshape(F * cells, C) for g in groups], 1
        )
        res = dot(gt[...], rhs, 1, 0)
        for n, g in enumerate(groups):
            for c in range(3):
                for sp in range(S):
                    acc[sp % 2, g, sp // 2, :, c * C : (c + 1) * C] = res[
                        c * C + sp * oc : c * C + (sp + 1) * oc, n * C : (n + 1) * C
                    ]
        for u, (lo, hi) in enumerate(units):
            if max(order.index(g) for g in range(lo, hi)) in [order.index(g) for g in groups]:
                core_copy(u).start()

    half_lane = lax.broadcasted_iota(jnp.int32, (oc // 2, 128), 1) < 64
    arrived = set()

    def fold_core(c):
        for u, (lo, hi) in enumerate(units):
            if u not in arrived and any(lo <= g < hi for g in groups_of(c)):
                core_copy(u).wait_recv()
                arrived.add(u)
        for yy in range(Y):
            for xx in range(X):
                off = (c * X + xx) * KT
                base = off // 128 * 128
                wide = min(-(-KT // 128) * 128 + 128, KC - base)
                win = jnp.concatenate(
                    [
                        acc[core, k // 3, yy, :, k % 3 * C : (k % 3 + 1) * C]
                        + recv1[k // 3, yy, :, k % 3 * C : (k % 3 + 1) * C]
                        for k in range(base // C, (base + wide) // C)
                    ],
                    1,
                )
                if off > base:
                    win = pltpu.roll(win, wide - (off - base), 1)
                pieces = [win[:, 128 * k : 128 * (k + 1)] for k in range(full)]
                if rest:
                    last = win[:, 128 * full : 128 * (full + 1)]
                    if folded:
                        last = jnp.where(
                            half_lane, last[: oc // 2], pltpu.roll(last[oc // 2 :], 64, 1)
                        )
                    pieces.append(last)
                block = jnp.concatenate(pieces, 0)
                sum2[c, yy, xx] = block
                stage2[yy, xx, c] = block.astype(link_type)
        for k, (lo, hi) in enumerate(spans):
            if c == hi - 1:
                for dy, dx in peers:
                    plane_copy(k, dy, dx).start()

    def fold_plane(c):
        v = sum2[c, y, x]
        for k, (lo, hi) in enumerate(spans):
            if c == lo:
                for dy, dx in peers:
                    plane_copy(k, dy, dx).wait_recv()
        for dy, dx in peers:
            v = v + recv2[dy * X + dx, c].astype(f32)
        own3[c] = v
        stage3[c] = v.astype(link_type)
        start_if(z != c, z_copy(c, z))

    waiting = list(chunks)
    for n, groups in enumerate(sets):
        products(groups)
        if n == 1:
            proj_part = dot(step, pooled, 1, 0, highest)
            bias_part = dot(jnp.ones((8, W), f32), bias_sum, 1, 1, highest)
            sm_send[...] = jnp.where(lax.broadcasted_iota(jnp.int32, (8, C), 0) == L, bias_part, proj_part)
            for k in range(len(plane)):
                small_plane(k).start()
        known = sum((sets[k] for k in range(n + 1 - 1)), [])
        while waiting and all(g in known for g in groups_of(waiting[0])):
            fold_core(waiting.pop(0))
    for c in waiting:
        fold_core(c)

    sm = sm_send[...]
    for k in range(len(plane)):
        small_plane(k).wait_recv()
        sm = sm + sm_recv[k]
    sz_send[...] = sm
    for d in range(1, Z):
        small_z(d).start()
    for c in chunks:
        fold_plane(c)
    for d in range(1, Z):
        small_z(d).wait_recv()
        sm = sm + sz_recv[d]
    small_out[...] = sm

    res = own3[z]
    for d in range(1, Z):
        src = lax.rem(z + d, Z)
        z_copy(src, src).wait_recv()
        res = res + recv3[src].astype(f32)
    for k in range(full):
        weight_out[:, 128 * k : 128 * (k + 1)] = res[k * oc : (k + 1) * oc]
    if rest:
        last = res[full * oc :]
        if folded:
            last = jnp.concatenate([last, pltpu.roll(last, 64, 1)], 0)
        weight_out[:, 128 * full :] = last[:, :rest]

    sent_if(up_s, row_up)
    sent_if(dn_s, row_dn)
    sent_if(up_t, inner)
    sent_if(late_dn, pass_dn)
    sent_if(late_up, pass_up)
    for d in range(1, X):
        cgx_copy(d).wait_send()
    for d in range(1, Z):
        cgz_copy(d).wait_send()
        small_z(d).wait_send()
    for k in range(len(plane)):
        small_plane(k).wait_send()
    for u in range(len(units)):
        core_copy(u).wait_send()
    for k in range(len(spans)):
        for dy, dx in peers:
            plane_copy(k, dy, dx).wait_send()
    for c in range(Z):
        sent_if(z != c, z_copy(c, z))


def finish_kernel(quant, wg, small, quant_out, weight_out, proj_out, bias_out):
    L = proj_out.shape[0]
    quant_out[...] = quant[...]
    weight_out[...] = wg[...]
    proj_out[...] = small[0:L]
    bias_out[...] = small[L : L + 1]


def on_device(T, S, frames, conv_weight, conv_bias, projection, levels, centres, code_grad):
    F, R, W, C = frames.shape
    KC = conv_weight.shape[0]
    KT = KC // T
    oc, Y, cells = C // S, S // 2, R * W
    Z, X = grid_of(T)
    PB = packed_rows(oc, KT)[3]
    L, TILE = levels.shape[0], code_grad.shape[2]
    scale = float(F * T * R * S * W) ** -0.5
    vmem = pl.BlockSpec(memory_space=pltpu.VMEM)
    dma = pltpu.SemaphoreType.DMA
    held = pl.pallas_call(
        functools.partial(block_kernel, T, S, scale),
        out_shape=(
            pltpu.VMEM((oc, KT), f32),
            pltpu.VMEM((8, C), f32),
            pltpu.VMEM(centres.shape, f32),
        ),
        in_specs=[pl.BlockSpec(memory_space=pl.ANY)] * 7,
        out_specs=(vmem,) * 3,
        scratch_shapes=[
            pltpu.VMEM(centres.shape, jnp.int32),
            pltpu.VMEM((F + 2, R + 2, W, C), bf16),
            pltpu.VMEM((KC, C), bf16),
            pltpu.VMEM((1, C), f32),
            pltpu.VMEM((L, C), f32),
            pltpu.SMEM((L,), jnp.int32),
            pltpu.VMEM((T, R, TILE), f32),
            pltpu.VMEM((Z, X, 8, 128), f32),
            pltpu.VMEM((X, Z, 8, 128), f32),
            pltpu.VMEM((Z, X, 8, 128), f32),
            pltpu.VMEM((8, C), f32),
            pltpu.VMEM((2, cells, 3 * C), f32),
            pltpu.VMEM((F * R, C, W), f32),
            pltpu.VMEM((3 * C, F * cells), bf16),
            pltpu.VMEM((2, 9, Y, oc, 3 * C), f32),
            pltpu.VMEM((9, Y, oc, 3 * C), f32),
            pltpu.VMEM((Z, Y, X, PB, 128), f32),
            pltpu.VMEM((Y, X, Z, PB, 128), link_type),
            pltpu.VMEM((Y * X, Z, PB, 128), link_type),
            pltpu.VMEM((Z, PB, 128), f32),
            pltpu.VMEM((Z, PB, 128), link_type),
            pltpu.VMEM((Z, PB, 128), link_type),
            pltpu.VMEM((8, C), f32),
            pltpu.VMEM((S * X, 8, C), f32),
            pltpu.VMEM((8, C), f32),
            pltpu.VMEM((Z, 8, C), f32),
            dma((9,)), pltpu.SemaphoreType.REGULAR((max(Z - 2, 1), 2)),
            dma((7,)), dma((7,)), dma((X,)), dma((X,)), dma((Z,)), dma((Z,)),
            dma((S * X,)), dma((S * X,)), dma((Z,)), dma((Z,)),
            dma((9,)), dma((9,)), dma((Z, Y * X)), dma((Z, Y * X)), dma((Z,)), dma((Z,)),
        ],
        compiler_params=pltpu.CompilerParams(
            collective_id=0, has_side_effects=True, vmem_limit_bytes=56 * 1024 * 1024
        ),
    )(frames, conv_weight, conv_bias.reshape(1, C), projection.T, levels, code_grad, centres)
    wg, small, quantized = (
        pltpu.with_memory_space_constraint(v, pltpu.VMEM) for v in held
    )
    quantized, wg, proj_grad, bias_grad = pl.pallas_call(
        finish_kernel,
        out_shape=(
            jax.ShapeDtypeStruct(centres.shape, f32),
            jax.ShapeDtypeStruct(wg.shape, f32),
            jax.ShapeDtypeStruct((L, C), f32),
            jax.ShapeDtypeStruct((1, C), f32),
        ),
        in_specs=[vmem] * 3,
        out_specs=(vmem,) * 4,
    )(quantized, wg, small)
    return quantized, wg.T, proj_grad.T, bias_grad.reshape(C)


def solution(mesh):
    return jax.shard_map(
        functools.partial(on_device, mesh.shape["tm"], mesh.shape["space"]),
        mesh=mesh,
        in_specs=(
            P("tm", "space", None, None),
            P(),
            P(),
            P(),
            P(),
            P(None, "space", "tm"),
            P(None, "space", "tm"),
        ),
        out_specs=(P(None, "space", "tm"), P("tm", "space"), P(), P()),
        check_vma=False,
    )
```

```python
import functools

import jax
import jax.numpy as jnp
from jax import lax
from jax.experimental import pallas as pl
from jax.experimental.pallas import tpu as pltpu
from jax.sharding import PartitionSpec as P

offset_scale = 0.45
commit_weight = 0.25
highest = lax.Precision.HIGHEST
MESH = pl.DeviceIdType.MESH
f32, bf16 = jnp.float32, jnp.bfloat16
link_type = bf16


def dot(a, b, ca, cb, precision=None):
    return lax.dot_general(
        a, b, (((ca,), (cb,)), ((), ())), preferred_element_type=f32, precision=precision
    )


def per_level(levels_ref, index, count):
    half = jnp.ones(index.shape, f32)
    for j in range(count):
        half = jnp.where(index == j, (levels_ref[j].astype(f32) - 1.0) * 0.5, half)
    return half


def grid_of(T):
    X = max(d for d in range(1, T + 1) if T % d == 0 and d * d <= T)
    return T // X, X


def packed_rows(oc, KT):
    full, rest = KT // 128, KT % 128
    folded = 0 < rest <= 64 and oc % 32 == 0
    return full, rest, folded, full * oc + (oc // 2 if folded else oc if rest else 0)


def block_kernel(
    T, S, scale,
    frames, weight_in, bias_in, proj_in, levels_in, code_in, centres_in,
    weight_out, small_out, quant_out,
    centres, xb, weight, bias, proj, levels, code_grad, cg_a, cg_b, cg_c, pscr, part, slope_t, gt, acc, recv1,
    sum2, stage2, recv2, own3, stage3, recv3,
    sm_send, sm_recv, sz_send, sz_recv,
    local_sem, token, halo_s, halo_r, cx_s, cx_r, cz_s, cz_r, ss_s, ss_r, sz_s, sz_r,
    core_s, core_r, y_s, y_r, tm_s, tm_r,
):
    Y = S // 2
    Z, X = grid_of(T)
    F, R, W, C = frames.shape
    L = levels_in.shape[0]
    TILE = code_in.shape[2]
    oc = C // S
    KC = weight_in.shape[0]
    KT = KC // T
    KZ = KT * X
    G = 3 * C
    full, rest, folded, PB = packed_rows(oc, KT)
    cells = R * W
    t = lax.axis_index("tm")
    s = lax.axis_index("space")
    y, core = s // 2, s % 2
    z, x = t // X, t % X
    up_t, dn_t, up_s, dn_s = t < T - 1, t > 0, s < S - 1, s > 0
    up_z, dn_z = z < Z - 1, z > 0
    turn_up = jnp.logical_and(up_t, x == X - 1)
    turn_dn = jnp.logical_and(dn_t, x == 0)

    barrier = pltpu.get_barrier_semaphore()

    def signal(tt, ss, sem=barrier):
        pl.semaphore_signal(sem, inc=1, device_id=(tt, ss), device_id_type=MESH)

    def signal_if(cond, tt, ss, sem=barrier):
        @pl.when(cond)
        def _():
            signal(tt, ss, sem)

    signal_if(turn_up, t + 1, s)
    signal_if(turn_dn, t - 1, s)
    signal_if(up_z, t + X, s)
    signal_if(dn_z, t - X, s)
    plane = [(dx, ds) for dx in range(X) for ds in range(S) if dx or ds]
    for dx, ds in plane:
        signal(z * X + lax.rem(x + dx, X), lax.rem(s + ds, S))

    own = pltpu.make_async_copy(frames, xb.at[2 : 2 + F, 1 : 1 + R], local_sem.at[0])
    first = [
        pltpu.make_async_copy(frames.at[0], xb.at[k, 1 : 1 + R], local_sem.at[1 + k])
        for k in range(2)
    ]
    code_load = pltpu.make_async_copy(code_in, code_grad, local_sem.at[3])
    proj_load = pltpu.make_async_copy(proj_in, proj, local_sem.at[4])
    bias_load = pltpu.make_async_copy(bias_in, bias, local_sem.at[5])
    levels_load = pltpu.make_async_copy(levels_in, levels, local_sem.at[6])
    weight_load = pltpu.make_async_copy(weight_in, weight, local_sem.at[7])
    centres_load = pltpu.make_async_copy(centres_in, centres, local_sem.at[8])
    code_load.start()
    own.start()
    weight_load.start()
    proj_load.start()
    bias_load.start()
    levels_load.start()
    centres_load.start()

    @pl.when(t == 0)
    def _():
        for copy in first:
            copy.start()

    cg_a[...] = jnp.zeros_like(cg_a)
    pscr[...] = jnp.zeros_like(pscr)

    @pl.when(s == 0)
    def _():
        xb[:, 0] = jnp.zeros((F + 2, W, C), bf16)

    @pl.when(s == S - 1)
    def _():
        xb[:, R + 1] = jnp.zeros((F + 2, W, C), bf16)

    code_load.wait()
    for k in range(T):
        cg_a[k // X, k % X, 0:R, 0:TILE] = code_grad[k]
    cg_b[0] = cg_a[:, x]

    one = lambda c: jnp.where(c, 1, 0)
    pl.semaphore_wait(
        barrier,
        (S * X - 1) + one(up_z) + one(dn_z) + one(turn_up) + one(turn_dn),
    )

    def remote(src, dst, ss_, rs_, tt, sp):
        return pltpu.make_async_remote_copy(
            src_ref=src, dst_ref=dst, send_sem=ss_, recv_sem=rs_,
            device_id=(tt, sp), device_id_type=MESH,
        )

    def start_if(cond, copy):
        @pl.when(cond)
        def _():
            copy.start()

    def recv_if(cond, copy):
        @pl.when(cond)
        def _():
            copy.wait_recv()

    def sent_if(cond, copy):
        @pl.when(cond)
        def _():
            copy.wait_send()

    def cgx_copy(d):
        to = lax.rem(x + d, X)
        return remote(cg_a.at[:, to], cg_b.at[d], cx_s.at[d], cx_r.at[d], z * X + to, s)

    def cgz_copy(d):
        to = lax.rem(z + d, Z)
        return remote(cg_b.at[:, to], cg_c.at[d], cz_s.at[d], cz_r.at[d], to * X + x, s)

    H = R + 1

    def halo(k, src, dst, tt, sp):
        return remote(src, dst, halo_s.at[k], halo_r.at[k], tt, sp)

    row_up = halo(0, frames.at[:, R - 1], xb.at[2 : 2 + F, 0], t, s + 1)
    row_dn = halo(1, frames.at[:, 0], xb.at[2 : 2 + F, H], t, s - 1)
    edge_lo = halo(2, frames.at[F - 2 : F, 0], xb.at[0:2, 1], t + 1, s)
    edge_hi = halo(3, frames.at[F - 2 : F, R - 1], xb.at[0:2, R], t + 1, s)
    inner = halo(4, frames.at[F - 2 : F, 1 : R - 1], xb.at[0:2, 2:R], t + 1, s)
    pass_dn = halo(5, xb.at[0:2, 1], xb.at[0:2, H], t, s - 1)
    pass_up = halo(6, xb.at[0:2, R], xb.at[0:2, 0], t, s + 1)
    late_dn, late_up = jnp.logical_and(dn_t, dn_s), jnp.logical_and(dn_t, up_s)

    rounds = max(Z - 2, 0)

    def chain(side):
        sends, gets, to = ((up_z, dn_z, t + X), (dn_z, up_z, t - X))[side]
        for r in range(rounds):
            @pl.when(gets)
            def _():
                pl.semaphore_wait(token.at[r, side], 1)

            if r + 1 < rounds:
                signal_if(sends, to, s, token.at[r + 1, side])

    def cgz_start(upper):
        for d in range(1, Z):
            above = lax.rem(z + d, Z) > z
            start_if(above if upper else jnp.logical_not(above), cgz_copy(d))

    if rounds:
        signal_if(up_z, t + X, s, token.at[0, 0])
        signal_if(dn_z, t - X, s, token.at[0, 1])
    for d in range(1, X):
        cgx_copy(d).start()
    start_if(up_t, edge_lo)
    start_if(up_t, edge_hi)
    start_if(up_s, row_up)
    start_if(dn_s, row_dn)
    proj_load.wait()
    bias_load.wait()
    levels_load.wait()
    centres_load.wait()
    column = lax.broadcasted_iota(jnp.int32, centres.shape, 2)
    half = per_level(levels, lax.rem(column, L), L)
    quant_out[...] = (centres[...].astype(f32) - half) / half
    pscr[0:L] = proj[...]
    proj_t = pscr[...]
    def taps(jobs, times):
        slabs = []
        weights = []
        for a in times:
            for b in range(3):
                slabs.append(
                    jnp.concatenate(
                        [xb[f + a, lo + b : hi + b].reshape((hi - lo) * W, C) for f, lo, hi in jobs], 0
                    )
                )
                k0 = (a * 3 + b) * G
                weights.append(
                    jnp.concatenate([weight[k0 + c * C : k0 + (c + 1) * C] for c in range(3)], 1)
                )
        return dot(jnp.concatenate(slabs, 1), jnp.concatenate(weights, 0), 1, 0)

    sums = {}

    def rows_end(out, jobs):
        size = out.shape[0]
        row = lax.broadcasted_iota(jnp.int32, (size, C), 0) % W
        left = jnp.where(row == 0, 0.0, pltpu.roll(out[:, 0:C], 1, 0))
        right = jnp.where(row == W - 1, 0.0, pltpu.roll(out[:, 2 * C :], size - 1, 0))
        pre = out[:, C : 2 * C] + bias[...] + left + right
        sig = 1.0 / (1.0 + jnp.exp(-pre))
        act = (pre * sig).astype(bf16).astype(f32)
        slope = sig * (1.0 + pre * (1.0 - sig))
        lines = [(f, h) for f, lo, hi in jobs for h in range(lo, hi)]
        for n, (f, h) in enumerate(lines):
            slope_t[f * R + h] = slope[n * W : (n + 1) * W].T
            line = act[n * W : (n + 1) * W]
            sums[h] = sums[h] + line if h in sums else line

    inside = lambda f: [(f, 1, R - 1)]
    outside = lambda f: [(f, 0, 1), (f, R - 1, R)]

    def own_taps(place):
        for k, times in ((0, (2,)), (1, (1, 2))):
            out = taps(place(k), times)
            at = 0
            for _, lo, hi in place(k):
                part[k, lo * W : hi * W] = out[at : at + (hi - lo) * W]
                at += (hi - lo) * W

    def frames_of(place):
        return sum((place(f) for f in range(2, F)), [])

    own.wait()
    weight_load.wait()
    rows_end(taps(frames_of(inside), (0, 1, 2)), frames_of(inside))
    own_taps(inside)
    sent_if(up_t, edge_lo)
    sent_if(up_t, edge_hi)
    start_if(up_t, inner)
    recv_if(dn_s, row_up)
    recv_if(up_s, row_dn)
    rows_end(taps(frames_of(outside), (0, 1, 2)), frames_of(outside))
    recv_if(dn_t, edge_lo)
    start_if(late_dn, pass_dn)
    recv_if(dn_t, edge_hi)
    start_if(late_up, pass_up)
    chain(0)
    for d in range(1, X):
        cgx_copy(d).wait_recv()
    cgz_start(False)
    chain(1)
    cgz_start(True)
    own_taps(outside)

    wt = TILE // L
    r_i = lax.broadcasted_iota(jnp.int32, (T * 8, cells), 0)
    q_i = lax.broadcasted_iota(jnp.int32, (T * 8, cells), 1)
    piece = r_i // 8
    owner = lax.rem(z - piece // X + Z, Z) * X + lax.rem(x - piece % X + X, X)
    pick = jnp.logical_and(r_i % 8 == q_i // W, owner == (q_i % W) // wt).astype(f32)
    l_i = lax.broadcasted_iota(jnp.int32, (128, cells), 0)
    w_i = lax.broadcasted_iota(jnp.int32, (128, cells), 1) % W
    keep = jnp.logical_and(l_i // L == w_i % wt, l_i < TILE)
    j_i = lax.broadcasted_iota(jnp.int32, (8, 128), 0)
    m_i = lax.broadcasted_iota(jnp.int32, (8, 128), 1)
    fold = jnp.logical_and(m_i % L == j_i, m_i < TILE).astype(f32)
    half_j = per_level(levels, lax.broadcasted_iota(jnp.int32, (8, cells), 0), L)

    @pl.when(t == 0)
    def _():
        for k in range(2):
            first[k].wait()
            xb[k, 0] = xb[2, 0]
            xb[k, H] = xb[2, H]

    recv_if(dn_t, inner)
    recv_if(late_up, pass_dn)
    recv_if(late_dn, pass_up)
    rows_end(part[0] + taps([(0, 0, R)], (0, 1)), [(0, 0, R)])
    rows_end(part[1] + taps([(1, 0, R)], (0,)), [(1, 0, R)])
    pooled = jnp.concatenate([sums[h] for h in range(R)], 0) * 0.25

    latent = dot(proj_t, pooled, 1, 1, highest)
    squashed = jnp.tanh(latent)
    cg_c[0] = cg_b[:, z]
    for d in range(1, Z):
        cgz_copy(d).wait_recv()
    cg_all = cg_c[...].reshape(T * 8, 128)
    spread = dot(cg_all, pick, 0, 0, highest)
    spread = jnp.where(keep, spread, 0.0)
    code = dot(fold, spread, 1, 0, highest)
    code = code / half_j

    step = (
        (code + 2.0 * commit_weight * offset_scale * squashed)
        * offset_scale
        * (1.0 - squashed * squashed)
        * scale
    )
    pg_t = dot(proj_t, step, 0, 0, highest) * 0.25

    lane = lax.broadcasted_iota(jnp.int32, (C, W), 1)
    bias_sum = jnp.zeros((C, W), f32)
    for f in range(F):
        for h in range(R):
            g = pg_t[:, h * W : (h + 1) * W] * slope_t[f * R + h]
            bias_sum = bias_sum + g
            q0 = (f * R + h) * W
            gt[0:C, q0 : q0 + W] = jnp.where(lane == W - 1, 0.0, pltpu.roll(g, W - 1, 1)).astype(bf16)
            gt[C : 2 * C, q0 : q0 + W] = g.astype(bf16)
            gt[2 * C :, q0 : q0 + W] = jnp.where(lane == 0, 0.0, pltpu.roll(g, 1, 1)).astype(bf16)

    def small_plane(k):
        dx, ds = plane[k]
        return remote(
            sm_send, sm_recv.at[k], ss_s.at[k], ss_r.at[k],
            z * X + lax.rem(x + dx, X), lax.rem(s + ds, S),
        )

    def small_z(d):
        return remote(sz_send, sz_recv.at[d], sz_s.at[d], sz_r.at[d], lax.rem(z + d, Z) * X + x, s)


    def core_copy(g):
        lo, hi = units[g]
        return remote(
            acc.at[1 - core, lo:hi], recv1.at[lo:hi], core_s.at[g], core_r.at[g],
            t, s + 1 - 2 * core,
        )

    def groups_of(c):
        return range(c * KZ // G, ((c + 1) * KZ - 1) // G + 1)

    chunks = sorted(range(Z), key=lambda c: -max(c, Z - 1 - c))
    order, units = [], []
    for c in chunks:
        fresh = [g for g in groups_of(c) if g not in order]
        order += fresh
        if fresh:
            units.append((fresh[0], fresh[-1] + 1))
    sets = [order[k : k + 2] for k in range(0, len(order), 2)]

    spans = [(c, c + 1) for c in range(Z)]

    def plane_copy(c, dy, dx):
        ty, tx, k = lax.rem(y + dy, Y), lax.rem(x + dx, X), dy * X + dx
        lo, hi = spans[c]
        return remote(
            stage2.at[ty, tx, lo:hi], recv2.at[k, lo:hi], y_s.at[c, k], y_r.at[c, k],
            z * X + tx, ty * 2 + core,
        )

    def z_copy(to, slot):
        return remote(stage3.at[to], recv3.at[slot], tm_s.at[to], tm_r.at[slot], to * X + x, s)

    peers = [(dy, dx) for dy in range(Y) for dx in range(X) if dy or dx]
    def products(groups):
        rhs = jnp.concatenate(
            [xb[g // 3 : g // 3 + F, g % 3 : g % 3 + R].reshape(F * cells, C) for g in groups], 1
        )
        res = dot(gt[...], rhs, 1, 0)
        for n, g in enumerate(groups):
            for c in range(3):
                for sp in range(S):
                    acc[sp % 2, g, sp // 2, :, c * C : (c + 1) * C] = res[
                        c * C + sp * oc : c * C + (sp + 1) * oc, n * C : (n + 1) * C
                    ]
        for u, (lo, hi) in enumerate(units):
            if max(order.index(g) for g in range(lo, hi)) in [order.index(g) for g in groups]:
                core_copy(u).start()

    half_lane = lax.broadcasted_iota(jnp.int32, (oc // 2, 128), 1) < 64
    arrived = set()

    def fold_core(c):
        for u, (lo, hi) in enumerate(units):
            if u not in arrived and any(lo <= g < hi for g in groups_of(c)):
                core_copy(u).wait_recv()
                arrived.add(u)
        for yy in range(Y):
            for xx in range(X):
                off = (c * X + xx) * KT
                base = off // 128 * 128
                wide = min(-(-KT // 128) * 128 + 128, KC - base)
                win = jnp.concatenate(
                    [
                        acc[core, k // 3, yy, :, k % 3 * C : (k % 3 + 1) * C]
                        + recv1[k // 3, yy, :, k % 3 * C : (k % 3 + 1) * C]
                        for k in range(base // C, (base + wide) // C)
                    ],
                    1,
                )
                if off > base:
                    win = pltpu.roll(win, wide - (off - base), 1)
                pieces = [win[:, 128 * k : 128 * (k + 1)] for k in range(full)]
                if rest:
                    last = win[:, 128 * full : 128 * (full + 1)]
                    if folded:
                        last = jnp.where(
                            half_lane, last[: oc // 2], pltpu.roll(last[oc // 2 :], 64, 1)
                        )
                    pieces.append(last)
                block = jnp.concatenate(pieces, 0)
                sum2[c, yy, xx] = block
                stage2[yy, xx, c] = block.astype(link_type)
        for k, (lo, hi) in enumerate(spans):
            if c == hi - 1:
                for dy, dx in peers:
                    plane_copy(k, dy, dx).start()

    def fold_plane(c):
        v = sum2[c, y, x]
        for k, (lo, hi) in enumerate(spans):
            if c == lo:
                for dy, dx in peers:
                    plane_copy(k, dy, dx).wait_recv()
        for dy, dx in peers:
            v = v + recv2[dy * X + dx, c].astype(f32)
        own3[c] = v
        stage3[c] = v.astype(link_type)
        start_if(z != c, z_copy(c, z))

    waiting = list(chunks)
    for n, groups in enumerate(sets):
        products(groups)
        if n == 1:
            proj_part = dot(step, pooled, 1, 0, highest)
            bias_part = dot(jnp.ones((8, W), f32), bias_sum, 1, 1, highest)
            sm_send[...] = jnp.where(lax.broadcasted_iota(jnp.int32, (8, C), 0) == L, bias_part, proj_part)
            for k in range(len(plane)):
                small_plane(k).start()
        known = sum((sets[k] for k in range(n + 1 - 1)), [])
        while waiting and all(g in known for g in groups_of(waiting[0])):
            fold_core(waiting.pop(0))
    for c in waiting:
        fold_core(c)

    sm = sm_send[...]
    for k in range(len(plane)):
        small_plane(k).wait_recv()
        sm = sm + sm_recv[k]
    sz_send[...] = sm
    for d in range(1, Z):
        small_z(d).start()
    for c in chunks:
        fold_plane(c)
    for d in range(1, Z):
        small_z(d).wait_recv()
        sm = sm + sz_recv[d]
    small_out[...] = sm

    res = own3[z]
    for d in range(1, Z):
        src = lax.rem(z + d, Z)
        z_copy(src, src).wait_recv()
        res = res + recv3[src].astype(f32)
    for k in range(full):
        weight_out[:, 128 * k : 128 * (k + 1)] = res[k * oc : (k + 1) * oc]
    if rest:
        last = res[full * oc :]
        if folded:
            last = jnp.concatenate([last, pltpu.roll(last, 64, 1)], 0)
        weight_out[:, 128 * full :] = last[:, :rest]

    sent_if(up_s, row_up)
    sent_if(dn_s, row_dn)
    sent_if(up_t, inner)
    sent_if(late_dn, pass_dn)
    sent_if(late_up, pass_up)
    for d in range(1, X):
        cgx_copy(d).wait_send()
    for d in range(1, Z):
        cgz_copy(d).wait_send()
        small_z(d).wait_send()
    for k in range(len(plane)):
        small_plane(k).wait_send()
    for u in range(len(units)):
        core_copy(u).wait_send()
    for k in range(len(spans)):
        for dy, dx in peers:
            plane_copy(k, dy, dx).wait_send()
    for c in range(Z):
        sent_if(z != c, z_copy(c, z))


def finish_kernel(quant, wg, small, quant_out, weight_out, proj_out, bias_out):
    L = proj_out.shape[0]
    quant_out[...] = quant[...]
    weight_out[...] = wg[...]
    proj_out[...] = small[0:L]
    bias_out[...] = small[L : L + 1]


def on_device(T, S, frames, conv_weight, conv_bias, projection, levels, centres, code_grad):
    F, R, W, C = frames.shape
    KC = conv_weight.shape[0]
    KT = KC // T
    oc, Y, cells = C // S, S // 2, R * W
    Z, X = grid_of(T)
    PB = packed_rows(oc, KT)[3]
    L, TILE = levels.shape[0], code_grad.shape[2]
    scale = float(F * T * R * S * W) ** -0.5
    vmem = pl.BlockSpec(memory_space=pltpu.VMEM)
    dma = pltpu.SemaphoreType.DMA
    held = pl.pallas_call(
        functools.partial(block_kernel, T, S, scale),
        out_shape=(
            pltpu.VMEM((oc, KT), f32),
            pltpu.VMEM((8, C), f32),
            pltpu.VMEM(centres.shape, f32),
        ),
        in_specs=[pl.BlockSpec(memory_space=pl.ANY)] * 7,
        out_specs=(vmem,) * 3,
        scratch_shapes=[
            pltpu.VMEM(centres.shape, jnp.int32),
            pltpu.VMEM((F + 2, R + 2, W, C), bf16),
            pltpu.VMEM((KC, C), bf16),
            pltpu.VMEM((1, C), f32),
            pltpu.VMEM((L, C), f32),
            pltpu.SMEM((L,), jnp.int32),
            pltpu.VMEM((T, R, TILE), f32),
            pltpu.VMEM((Z, X, 8, 128), f32),
            pltpu.VMEM((X, Z, 8, 128), f32),
            pltpu.VMEM((Z, X, 8, 128), f32),
            pltpu.VMEM((8, C), f32),
            pltpu.VMEM((2, cells, 3 * C), f32),
            pltpu.VMEM((F * R, C, W), f32),
            pltpu.VMEM((3 * C, F * cells), bf16),
            pltpu.VMEM((2, 9, Y, oc, 3 * C), f32),
            pltpu.VMEM((9, Y, oc, 3 * C), f32),
            pltpu.VMEM((Z, Y, X, PB, 128), f32),
            pltpu.VMEM((Y, X, Z, PB, 128), link_type),
            pltpu.VMEM((Y * X, Z, PB, 128), link_type),
            pltpu.VMEM((Z, PB, 128), f32),
            pltpu.VMEM((Z, PB, 128), link_type),
            pltpu.VMEM((Z, PB, 128), link_type),
            pltpu.VMEM((8, C), f32),
            pltpu.VMEM((S * X, 8, C), f32),
            pltpu.VMEM((8, C), f32),
            pltpu.VMEM((Z, 8, C), f32),
            dma((9,)), pltpu.SemaphoreType.REGULAR((max(Z - 2, 1), 2)),
            dma((7,)), dma((7,)), dma((X,)), dma((X,)), dma((Z,)), dma((Z,)),
            dma((S * X,)), dma((S * X,)), dma((Z,)), dma((Z,)),
            dma((9,)), dma((9,)), dma((Z, Y * X)), dma((Z, Y * X)), dma((Z,)), dma((Z,)),
        ],
        compiler_params=pltpu.CompilerParams(
            collective_id=0, has_side_effects=True, vmem_limit_bytes=56 * 1024 * 1024
        ),
    )(frames, conv_weight, conv_bias.reshape(1, C), projection.T, levels, code_grad, centres)
    wg, small, quantized = (
        pltpu.with_memory_space_constraint(v, pltpu.VMEM) for v in held
    )
    quantized, wg, proj_grad, bias_grad = pl.pallas_call(
        finish_kernel,
        out_shape=(
            jax.ShapeDtypeStruct(centres.shape, f32),
            jax.ShapeDtypeStruct(wg.shape, f32),
            jax.ShapeDtypeStruct((L, C), f32),
            jax.ShapeDtypeStruct((1, C), f32),
        ),
        in_specs=[vmem] * 3,
        out_specs=(vmem,) * 4,
    )(quantized, wg, small)
    return quantized, wg.T, proj_grad.T, bias_grad.reshape(C)


def solution(mesh):
    return jax.shard_map(
        functools.partial(on_device, mesh.shape["tm"], mesh.shape["space"]),
        mesh=mesh,
        in_specs=(
            P("tm", "space", None, None),
            P(),
            P(),
            P(),
            P(),
            P(None, "space", "tm"),
            P(None, "space", "tm"),
        ),
        out_specs=(P(None, "space", "tm"), P("tm", "space"), P(), P()),
        check_vma=False,
    )
```
